32 devices in a mesh: ka: 8 (over z, y), col: 4 (over x, core).
Axes of the slice: x: 2, y: 2, z: 4, core: 2. Of those that a mesh axis runs over, the one named last changes fastest.
Arguments:
- amps: bfloat16 [16, 256, 192], P('ka', 'col'), may hold values from -6 to 6
- isdf_coeffs: bfloat16 [16, 2048, 256], P('ka', 'col'), may hold values from -0.375 to 0.375
- w_screen: bfloat16 [16, 2048, 2048], P(None, 'ka', 'col'), as said below
- energies: float32 [16, 256], P('ka', 'col'), may hold values from 0.5 to 3
- qsel: int32 [2], replicated, may hold values from 0 to 15
- partner: int32 [2, 16], replicated, may hold values from 0 to 15, each once within a row
Outputs:
- applied: float32 [16, 256, 192], P('ka', 'col')
The draws below stay inside these ranges and needn't reach their ends.
Inputs may be any that keep to these rules, and one draw needn't show every extreme that they name: Each row of partner is a permutation of the 16 k points. `w_screen`: each of the 16 matrices is symmetric.
All inputs are finite; a program needn't handle non-finite values.
Results may differ from the reference program's by a relative error of at most 0.013.
Values may be sent and summed in bfloat16 or wider, within the bound.
A program may use at most 64 MiB of HBM per device.

```python
import math
import jax
import jax.numpy as jnp
from jax import lax

NMU = 2048
NPAIR = 256
NEXC = 192
NQW = 16
NK = 16
N_COL = 4


def draw_w_screen(key, part):
    normals = jax.random.normal(jax.random.fold_in(key, 11), (NQW, NMU, NMU), jnp.float32)
    matrix = (normals + jnp.swapaxes(normals, 1, 2)) * (0.6 / (2.0 * NMU) ** 0.5)
    return matrix.astype(jnp.bfloat16)


def block_scale(own_key, dims, pieces, least, largest):
    def one(axis_at, blocks):
        heights = jax.random.uniform(jax.random.fold_in(jax.random.fold_in(own_key, 6), axis_at), (blocks,), jnp.float32, least / len(pieces), largest / len(pieces))
        return jnp.repeat(jnp.exp(heights), dims[axis_at] // blocks).reshape((-1,) + (1,) * (len(dims) - axis_at - 1))

    loudness = one(*pieces[0])
    for cut in pieces[1:]:
        loudness = loudness * one(*cut)
    return loudness


def noise(stream_key, shape, deviation, most, cuts=(), held_as=jnp.bfloat16):
    values = deviation * jax.random.normal(stream_key, shape, jnp.float32)
    if cuts:
        values = values * block_scale(stream_key, shape, cuts, -0.22, 0.18)
    return jnp.clip(values, -most, most).astype(held_as)


def setup_inputs(seed: int = 0) -> dict:
    streams_of = jax.random.split(jax.random.key(seed), 7)
    amps = noise(streams_of[0], (NK, NPAIR, NEXC), 1.0, 6.0, ((0, 8), (1, 4)))
    isdf_coeffs = noise(streams_of[1], (NK, NMU, NPAIR), NPAIR ** -0.5, 0.375, ((0, 8), (1, 4)))
    w_screen = draw_w_screen(jax.random.fold_in(streams_of[6], 71), 0)
    energies = jnp.clip(jnp.exp(math.log(3.0) - 1.7917595 * jax.random.uniform(streams_of[3], (NK, NPAIR), jnp.float32) ** block_scale(streams_of[3], (NK, NPAIR), ((0, 8), (1, 4)), -0.2, 0.2)), 0.5, 3.0)
    qsel = jax.random.randint(streams_of[4], (2,), 0, NQW).astype(jnp.int32)
    partner = jax.vmap(lambda own: jax.random.permutation(own, NK))(jax.random.split(streams_of[5], 2)).reshape((2, NK)).astype(jnp.int32)
    return dict(amps=amps, isdf_coeffs=isdf_coeffs, w_screen=w_screen, energies=energies, qsel=qsel, partner=partner)


def reference(amps, isdf_coeffs, w_screen, energies, qsel, partner):
    high = lax.Precision.HIGHEST
    block_rows = NMU // N_COL
    screens = [jnp.take(w_screen, qsel[shift], axis=0).astype(jnp.float32) for shift in range(2)]

    def per_point(index):
        coeffs_k = isdf_coeffs[index].astype(jnp.float32)
        total = energies[index][:, None] * amps[index].astype(jnp.float32)
        for shift in range(2):
            partner_amps = jnp.take(amps, partner[shift, index], axis=0).astype(jnp.float32)
            densities = jnp.dot(coeffs_k, partner_amps, precision=high).astype(jnp.bfloat16).astype(jnp.float32)
            screened = jnp.zeros((NMU, NEXC), jnp.float32)
            for block in range(N_COL):
                lower = block * block_rows
                upper = lower + block_rows
                partial_part = jnp.dot(screens[shift][:, lower:upper], densities[lower:upper], precision=high)
                partial_part = lax.optimization_barrier(partial_part.astype(jnp.bfloat16)).astype(jnp.float32)
                screened = screened + partial_part
            screened = screened.astype(jnp.bfloat16).astype(jnp.float32)
            total = total + jnp.dot(coeffs_k.T, screened, precision=high)
        return total

    return lax.map(per_point, jnp.arange(NK, dtype=jnp.int32))
```

```python
import functools

import jax
import jax.numpy as jnp
from jax import lax
from jax.experimental import pallas as pl
from jax.experimental.pallas import tpu as pltpu
from jax.sharding import PartitionSpec as P

MESH = pl.DeviceIdType.MESH
UP, DOWN, ACROSS = 0, 1, 2


def general_body(amps, isdf_coeffs, w_screen, energies, qsel, partner):
    k_local = amps.shape[0]
    vectors = amps.shape[2]
    offset_base = lax.axis_index("ka") * k_local
    owned = offset_base + jnp.arange(k_local, dtype=jnp.int32)
    wanted = jnp.take(partner, owned, axis=1).reshape(-1)
    everyone = lax.all_gather(amps, "ka", axis=0, tiled=True)
    picked = jnp.take(everyone, wanted, axis=0)
    partners = lax.all_gather(picked, "col", axis=1, tiled=True)
    partners = partners.reshape(2, k_local, partners.shape[1], vectors)
    densities = jnp.einsum(
        "kms,qkse->qmke", isdf_coeffs, partners, preferred_element_type=jnp.float32
    )
    width = densities.shape[1]
    densities = densities.astype(jnp.bfloat16).reshape(2, width, k_local * vectors)
    slabs = jnp.take(w_screen, qsel, axis=0)
    partials = jnp.einsum(
        "qrm,qmx->qrx",
        lax.all_gather(slabs, "ka", axis=1, tiled=True),
        densities,
        preferred_element_type=jnp.float32,
    )
    screened = lax.psum_scatter(
        partials.astype(jnp.bfloat16), "col", scatter_dimension=1, tiled=True
    ).astype(jnp.float32)
    screened = screened.astype(jnp.bfloat16).reshape(2, width, k_local, vectors)
    projected = jnp.einsum(
        "kms,qmke->kse", isdf_coeffs, screened, preferred_element_type=jnp.float32
    )
    summed = lax.psum_scatter(
        projected.astype(jnp.bfloat16), "col", scatter_dimension=1, tiled=True
    ).astype(jnp.float32)
    return summed + energies[:, :, None] * amps.astype(jnp.float32)


def listed(i, values):
    out = jnp.int32(values[0])
    for at, value in enumerate(values[1:], 1):
        out = jnp.where(i == at, jnp.int32(value), out)
    return out


def nt(a, b):
    return lax.dot_general(a, b, (((1,), (1,)), ((), ())), preferred_element_type=jnp.float32)


def nn(a, b):
    return jnp.dot(a, b, preferred_element_type=jnp.float32)


def kernel(
    n_ka, n_col, partner, amps, coeffs, w0, w1, out,
    abuf, pbuf, cbuf, wbuf, ebuf, xbuf, dens, bacc, proj, outgoing, incoming,
    a_send, a_recv, p_send, p_recv, c_send, c_recv, w_send, w_recv,
    e_send, e_recv, o_send, o_recv, own_sem,
):
    k_local, mine, vectors = amps.shape
    rows = w0.shape[0]
    me = lax.axis_index("ka")
    col = lax.axis_index("col")
    n_z = n_ka // 2
    z, y = lax.div(me, 2), lax.rem(me, 2)
    beside = me + 1 - 2 * y
    twin = col + 1 - 2 * lax.rem(col, 2)
    opposite = lax.rem(col + 2, n_col)
    corner = lax.rem(twin + 2, n_col)
    slabs = (w0, w1)

    def half_of(a):
        odd = lax.rem(a, 2)
        return jnp.where(a >= 2 * col, odd, 1 - odd)

    def remote(src, dst, send, recv, ka, at):
        return pltpu.make_async_remote_copy(
            src_ref=src, dst_ref=dst, send_sem=send, recv_sem=recv,
            device_id={"ka": ka, "col": at}, device_id_type=MESH,
        )

    barrier = pltpu.get_barrier_semaphore()
    for step in range(1, n_ka):
        pl.semaphore_signal(
            barrier, inc=1, device_id={"ka": lax.rem(me + step, n_ka), "col": col},
            device_id_type=MESH,
        )
    for step in range(1, n_col):
        pl.semaphore_signal(
            barrier, inc=1, device_id={"ka": me, "col": lax.rem(col + step, n_col)},
            device_id_type=MESH,
        )
    pl.semaphore_wait(barrier, n_ka + n_col - 2)

    slot = abuf.at[pl.ds(me * k_local, k_local)]
    amp_copies = []
    for step in range(1, n_ka):
        copy = remote(amps, slot, a_send.at[step], a_recv.at[step], lax.rem(me + step, n_ka), col)
        copy.start()
        amp_copies.append(copy)

    coeff_copies = []
    for k in range(k_local):
        for way, to in ((0, opposite), (1, twin)):
            copy = remote(
                coeffs.at[k], cbuf.at[col, k], c_send.at[way, k], c_recv.at[way, k], me, to
            )
            copy.start()
            coeff_copies.append(copy)

    def w_copy(way, source, j, own):
        to = (me + 2, me - 2, beside)[way]
        if own:
            src = slabs[j].at[:, pl.ds(pl.multiple_of(rows * half_of(me), rows), rows)]
        else:
            src = wbuf.at[source, j]
        return remote(src, wbuf.at[source, j], w_send.at[source, j, way], w_recv.at[source, j], to, col)

    def e_copy(way, j, own):
        to = (me + 2, me - 2, beside)[way]
        src = slabs[j].at[:, pl.ds(rows, rows)] if own else ebuf.at[j]
        return remote(src, ebuf.at[j], e_send.at[j, way], e_recv.at[j], to, col)

    def sends(source_z, go, own):
        source = source_z * 2 + y
        extra = (y == 0) & (source_z == col)
        up = (source_z <= z) & (z < n_z - 1)
        down = (source_z >= z) & (z > 0)
        for j in range(2):
            for way, wanted in ((UP, up), (DOWN, down), (ACROSS, None)):
                if wanted is None:
                    go(w_copy(way, source, j, own))
                else:
                    @pl.when(wanted)
                    def _(way=way, j=j):
                        go(w_copy(way, source, j, own))

        @pl.when(extra)
        def _():
            for j in range(2):
                for way, wanted in ((UP, up), (DOWN, down), (ACROSS, None)):
                    if wanted is None:
                        go(e_copy(way, j, own))
                    else:
                        @pl.when(wanted)
                        def _(way=way, j=j):
                            go(e_copy(way, j, own))

    def wait_block(source, is_extra):
        for j in range(2):
            w_copy(ACROSS, source, j, False).wait_recv()

        @pl.when(is_extra)
        def _():
            for j in range(2):
                e_copy(ACROSS, j, False).wait_recv()

    sends(z, lambda copy: copy.start(), True)

    local = [
        pltpu.make_async_copy(amps, slot, own_sem.at[0]),
        pltpu.make_async_copy(coeffs, cbuf.at[col], own_sem.at[1]),
    ]
    for j in range(2):
        local.append(
            pltpu.make_async_copy(
                slabs[j].at[:, pl.ds(pl.multiple_of(rows * half_of(me), rows), rows)],
                wbuf.at[me, j], own_sem.at[2 + j],
            )
        )
    for copy in local:
        copy.start()
    own_extra = [
        pltpu.make_async_copy(slabs[j].at[:, pl.ds(rows, rows)], ebuf.at[j], own_sem.at[4 + j])
        for j in range(2)
    ]

    @pl.when((y == 0) & (z == col))
    def _():
        for copy in own_extra:
            copy.start()
        for copy in own_extra:
            copy.wait()

    for copy in local:
        copy.wait()
    for copy in amp_copies:
        copy.wait_recv()

    for j in range(2):
        for k in range(k_local):
            at = partner[j, me * k_local + k]
            pbuf[j * k_local + k, pl.ds(pl.multiple_of(mine * col, mine), mine), :] = abuf[at]

    def nth(n):
        near = jnp.where(z < n_z - 1 - z, z, n_z - 1 - z)
        low = jnp.where(n <= near, near - n, n)
        return jnp.where(z < n_z - 1 - z, low, n_z - 1 - low)

    def relay(n):
        source_z = nth(n)
        wait_block(source_z * 2 + y, (y == 0) & (source_z == col))
        sends(source_z, lambda copy: copy.start(), False)

    pick_copies = []
    my_rows = pl.ds(pl.multiple_of(mine * col, mine), mine)
    for step in range(1, n_col):
        copy = remote(
            pbuf.at[:, my_rows], pbuf.at[:, my_rows],
            p_send.at[step], p_recv.at[step], me, lax.rem(col + step, n_col),
        )
        copy.start()
        pick_copies.append(copy)

    relay(1)

    corner_copies = []
    for k in range(k_local):
        coeff_copies[2 * k].wait_recv()
        copy = remote(
            cbuf.at[opposite, k], cbuf.at[opposite, k], c_send.at[2, k], c_recv.at[2, k], me, twin
        )
        copy.start()
        corner_copies.append(copy)
    for copy in pick_copies:
        copy.wait_recv()
    for j in range(2):
        for k in range(k_local):
            turned = pbuf[j * k_local + k].astype(jnp.float32).T.astype(jnp.bfloat16)
            xbuf[k, vectors * j : vectors * (j + 1), :] = turned
    proj[...] = jnp.zeros_like(proj)
    bacc[...] = jnp.zeros_like(bacc)
    for k in range(k_local):
        coeff_copies[2 * k + 1].wait_recv()
        corner_copies[k].wait_recv()

    relay(2)

    def coeff_rows(r, k):
        at = pl.ds(pl.multiple_of(rows * lax.rem(r, 2), rows), rows)
        return cbuf[lax.div(r, 2), k, at, :]

    @pl.loop(0, n_ka)
    def _(r):
        for k in range(k_local):
            both = nt(xbuf[k], coeff_rows(r, k)).astype(jnp.bfloat16)
            for j in range(2):
                dens[j, r, vectors * k : vectors * (k + 1), :] = both[vectors * j : vectors * (j + 1)]

    def project(part, r):
        low = part.astype(jnp.bfloat16)
        for k in range(k_local):
            proj[k] += nn(low[vectors * k : vectors * (k + 1)], coeff_rows(r, k))

    order = (0, 1, 0, 2, 1, 3, 2, 3)
    across = (0, 0, 1, 0, 1, 0, 1, 1)

    @pl.loop(0, n_ka)
    def _(i):
        @pl.when(i == 5)
        def _():
            relay(3)

        source_z = nth(listed(i, order))
        other = listed(i, across)
        source = source_z * 2 + jnp.where(other == 1, 1 - y, y)

        @pl.when(other == 1)
        def _():
            wait_block(source, (y == 1) & (source_z == col))

        half = half_of(source)
        b = 2 * col + half
        part = nt(dens[0, b], wbuf[source, 0]) + nt(dens[1, b], wbuf[source, 1])

        @pl.when(source_z == col)
        def _():
            bacc[half] += part

        @pl.when(source_z != col)
        def _():
            project(part, source)
            bacc[half] += nn(dens[0, source], wbuf[source, 0]) + nn(dens[1, source], wbuf[source, 1])

    bacc[0] += nt(dens[0, 2 * col + 1], ebuf[0]) + nt(dens[1, 2 * col + 1], ebuf[1])
    bacc[1] += nn(dens[0, 2 * col], ebuf[0]) + nn(dens[1, 2 * col], ebuf[1])
    for half in range(2):
        project(bacc[half], 2 * col + half)

    for k in range(k_local):
        turned = proj[k].T.astype(jnp.bfloat16)
        for c in range(n_col):
            outgoing[c, k] = turned[mine * c : mine * (c + 1)]
    out_copies = []
    for step in range(1, n_col):
        to = lax.rem(col + step, n_col)
        copy = remote(
            outgoing.at[to], incoming.at[step], o_send.at[step], o_recv.at[step], me, to
        )
        copy.start()
        out_copies.append(copy)
    total = outgoing[col].astype(jnp.float32)
    for step, copy in enumerate(out_copies, 1):
        copy.wait_recv()
        total += incoming[step].astype(jnp.float32)
    out[...] = total

    for copy in amp_copies + coeff_copies + pick_copies + corner_copies + out_copies:
        copy.wait_send()
    sends(z, lambda copy: copy.wait_send(), True)
    for n in range(1, n_z):
        sends(nth(n), lambda copy: copy.wait_send(), False)


def body(n_ka, n_col, amps, isdf_coeffs, w_screen, energies, qsel, partner):
    k_local, mine, vectors = amps.shape
    pairs = isdf_coeffs.shape[2]
    rows, width = w_screen.shape[1:]
    w0 = lax.dynamic_index_in_dim(w_screen, qsel[0], 0, keepdims=False)
    w1 = lax.dynamic_index_in_dim(w_screen, qsel[1], 0, keepdims=False)
    vmem = pl.BlockSpec(memory_space=pltpu.VMEM)
    dma = pltpu.SemaphoreType.DMA
    bf16, f32 = jnp.bfloat16, jnp.float32
    summed = pl.pallas_call(
        functools.partial(kernel, n_ka, n_col),
        out_shape=jax.ShapeDtypeStruct(amps.shape, f32),
        in_specs=[pl.BlockSpec(memory_space=pltpu.SMEM)] + [vmem] * 4,
        out_specs=vmem,
        scratch_shapes=[
            pltpu.VMEM((n_ka * k_local, mine, vectors), bf16),
            pltpu.VMEM((2 * k_local, pairs, vectors), bf16),
            pltpu.VMEM((n_col, k_local, width, pairs), bf16),
            pltpu.VMEM((n_ka, 2, rows, rows), bf16),
            pltpu.VMEM((2, rows, rows), bf16),
            pltpu.VMEM((k_local, 2 * vectors, pairs), bf16),
            pltpu.VMEM((2, n_ka, k_local * vectors, rows), bf16),
            pltpu.VMEM((2, k_local * vectors, rows), f32),
            pltpu.VMEM((k_local, vectors, pairs), f32),
            pltpu.VMEM((n_col, k_local, mine, vectors), bf16),
            pltpu.VMEM((n_col, k_local, mine, vectors), bf16),
            dma((n_ka,)), dma((n_ka,)),
            dma((n_col,)), dma((n_col,)),
            dma((3, k_local)), dma((3, k_local)),
            dma((n_ka, 2, 3)), dma((n_ka, 2)),
            dma((2, 3)), dma((2,)),
            dma((n_col,)), dma((n_col,)),
            dma((6,)),
        ],
        compiler_params=pltpu.CompilerParams(
            collective_id=0, has_side_effects=True, vmem_limit_bytes=48 * 2**20
        ),
    )(partner, amps, isdf_coeffs, w0, w1)
    return summed + energies[:, :, None] * amps.astype(f32)


def solution(mesh):
    placed = (
        P("ka", "col", None),
        P("ka", "col", None),
        P(None, "ka", "col"),
        P("ka", "col"),
        P(),
        P(),
    )
    n_ka, n_col = mesh.shape["ka"], mesh.shape["col"]
    paired = n_ka == 2 * n_col and n_col == 4
    chosen = functools.partial(body, n_ka, n_col) if paired else general_body
    return jax.shard_map(
        chosen, mesh=mesh, in_specs=placed, out_specs=P("ka", "col", None), check_vma=False
    )
```

```python
import functools

import jax
import jax.numpy as jnp
from jax import lax
from jax.experimental import pallas as pl
from jax.experimental.pallas import tpu as pltpu
from jax.sharding import PartitionSpec as P

MESH = pl.DeviceIdType.MESH
UP, DOWN, ACROSS = 0, 1, 2


def general_body(amps, isdf_coeffs, w_screen, energies, qsel, partner):
    k_local = amps.shape[0]
    vectors = amps.shape[2]
    offset_base = lax.axis_index("ka") * k_local
    owned = offset_base + jnp.arange(k_local, dtype=jnp.int32)
    wanted = jnp.take(partner, owned, axis=1).reshape(-1)
    everyone = lax.all_gather(amps, "ka", axis=0, tiled=True)
    picked = jnp.take(everyone, wanted, axis=0)
    partners = lax.all_gather(picked, "col", axis=1, tiled=True)
    partners = partners.reshape(2, k_local, partners.shape[1], vectors)
    densities = jnp.einsum(
        "kms,qkse->qmke", isdf_coeffs, partners, preferred_element_type=jnp.float32
    )
    width = densities.shape[1]
    densities = densities.astype(jnp.bfloat16).reshape(2, width, k_local * vectors)
    slabs = jnp.take(w_screen, qsel, axis=0)
    partials = jnp.einsum(
        "qrm,qmx->qrx",
        lax.all_gather(slabs, "ka", axis=1, tiled=True),
        densities,
        preferred_element_type=jnp.float32,
    )
    screened = lax.psum_scatter(
        partials.astype(jnp.bfloat16), "col", scatter_dimension=1, tiled=True
    ).astype(jnp.float32)
    screened = screened.astype(jnp.bfloat16).reshape(2, width, k_local, vectors)
    projected = jnp.einsum(
        "kms,qmke->kse", isdf_coeffs, screened, preferred_element_type=jnp.float32
    )
    summed = lax.psum_scatter(
        projected.astype(jnp.bfloat16), "col", scatter_dimension=1, tiled=True
    ).astype(jnp.float32)
    return summed + energies[:, :, None] * amps.astype(jnp.float32)


def listed(i, values):
    out = jnp.int32(values[0])
    for at, value in enumerate(values[1:], 1):
        out = jnp.where(i == at, jnp.int32(value), out)
    return out


def nt(a, b):
    return lax.dot_general(a, b, (((1,), (1,)), ((), ())), preferred_element_type=jnp.float32)


def nn(a, b):
    return jnp.dot(a, b, preferred_element_type=jnp.float32)


def kernel(
    n_ka, n_col, partner, amps, coeffs, slabs, out,
    abuf, pbuf, cbuf, wbuf, ebuf, xbuf, dens, bacc, proj, outgoing, incoming,
    a_send, a_recv, p_send, p_recv, c_send, c_recv, w_send, w_recv,
    e_send, e_recv, o_send, o_recv, own_sem,
):
    k_local, mine, vectors = amps.shape
    rows = slabs.shape[1]
    me = lax.axis_index("ka")
    col = lax.axis_index("col")
    n_z = n_ka // 2
    z, y = lax.div(me, 2), lax.rem(me, 2)
    beside = me + 1 - 2 * y
    twin = col + 1 - 2 * lax.rem(col, 2)
    opposite = lax.rem(col + 2, n_col)
    corner = lax.rem(twin + 2, n_col)

    def half_of(a):
        odd = lax.rem(a, 2)
        return jnp.where(a >= 2 * col, odd, 1 - odd)

    def remote(src, dst, send, recv, ka, at):
        return pltpu.make_async_remote_copy(
            src_ref=src, dst_ref=dst, send_sem=send, recv_sem=recv,
            device_id={"ka": ka, "col": at}, device_id_type=MESH,
        )

    barrier = pltpu.get_barrier_semaphore()
    for step in range(1, n_ka):
        pl.semaphore_signal(
            barrier, inc=1, device_id={"ka": lax.rem(me + step, n_ka), "col": col},
            device_id_type=MESH,
        )
    for step in range(1, n_col):
        pl.semaphore_signal(
            barrier, inc=1, device_id={"ka": me, "col": lax.rem(col + step, n_col)},
            device_id_type=MESH,
        )
    pl.semaphore_wait(barrier, n_ka + n_col - 2)

    slot = abuf.at[pl.ds(me * k_local, k_local)]
    amp_copies = []
    for step in range(1, n_ka):
        copy = remote(amps, slot, a_send.at[step], a_recv.at[step], lax.rem(me + step, n_ka), col)
        copy.start()
        amp_copies.append(copy)

    coeff_copies = []
    for k in range(k_local):
        for way, to in ((0, opposite), (1, twin)):
            copy = remote(
                coeffs.at[k], cbuf.at[col, k], c_send.at[way, k], c_recv.at[way, k], me, to
            )
            copy.start()
            coeff_copies.append(copy)

    def w_copy(way, source, j, own):
        to = (me + 2, me - 2, beside)[way]
        if own:
            src = slabs.at[j, :, pl.ds(pl.multiple_of(rows * half_of(me), rows), rows)]
        else:
            src = wbuf.at[source, j]
        return remote(src, wbuf.at[source, j], w_send.at[source, j, way], w_recv.at[source, j], to, col)

    own_extra_src = slabs.at[y, :, pl.ds(pl.multiple_of(rows * (1 - y), rows), rows)]

    def e_copy(way, j, own):
        to = (me + 2, me - 2, beside)[way]
        src = own_extra_src if own else ebuf.at[j]
        return remote(src, ebuf.at[j], e_send.at[j, way], e_recv.at[j], to, col)

    def across_first(source_z, j):
        return (source_z == 0) | (source_z == n_z - 1) if j == 1 else None

    def when(cond, act):
        if cond is None:
            act()
        else:
            pl.when(cond)(act)

    def sends(source_z, go, own):
        source = source_z * 2 + y
        extra = source_z == col
        up = (source_z <= z) & (z < n_z - 1)
        down = (source_z >= z) & (z > 0)
        for j in (1, 0):
            early = across_first(source_z, j)
            over = None if own or early is None else jnp.logical_not(early)
            for way, wanted in ((ACROSS, over), (UP, up), (DOWN, down)):
                when(wanted, lambda way=way, j=j: go(w_copy(way, source, j, own)))

        @pl.when(extra)
        def _():
            for way, wanted in ((ACROSS, None), (UP, up), (DOWN, down)):
                when(wanted, lambda way=way: go(e_copy(way, y, own)))

    def sends_other(source_z, go):
        source = source_z * 2 + 1 - y
        pl.when((source_z <= z) & (z < n_z - 1))(lambda: go(w_copy(UP, source, 1, False)))
        pl.when((source_z >= z) & (z > 0))(lambda: go(w_copy(DOWN, source, 1, False)))

    def wait_own(source_z):
        source = source_z * 2 + y
        for j in range(2):
            w_copy(ACROSS, source, j, False).wait_recv()
        pl.when(source_z == col)(lambda: e_copy(ACROSS, y, False).wait_recv())

    def wait_other(source_z):
        source = source_z * 2 + 1 - y
        w_copy(ACROSS, source, 0, False).wait_recv()
        pl.when(jnp.logical_not(across_first(source_z, 1)))(
            lambda: w_copy(ACROSS, source, 1, False).wait_recv()
        )
        pl.when(source_z == col)(lambda: e_copy(ACROSS, 1 - y, False).wait_recv())

    sends(z, lambda copy: copy.start(), True)

    local = [
        pltpu.make_async_copy(amps, slot, own_sem.at[0]),
        pltpu.make_async_copy(coeffs, cbuf.at[col], own_sem.at[1]),
    ]
    for j in range(2):
        local.append(
            pltpu.make_async_copy(
                slabs.at[j, :, pl.ds(pl.multiple_of(rows * half_of(me), rows), rows)],
                wbuf.at[me, j], own_sem.at[2 + j],
            )
        )
    for copy in local:
        copy.start()

    @pl.when(z == col)
    def _():
        copy = pltpu.make_async_copy(own_extra_src, ebuf.at[y], own_sem.at[4])
        copy.start()
        copy.wait()

    for copy in local:
        copy.wait()
    for copy in amp_copies:
        copy.wait_recv()

    for j in range(2):
        for k in range(k_local):
            at = partner[j, me * k_local + k]
            pbuf[j * k_local + k, pl.ds(pl.multiple_of(mine * col, mine), mine), :] = abuf[at]

    def nth(n):
        near = jnp.where(z < n_z - 1 - z, z, n_z - 1 - z)
        low = jnp.where(n <= near, near - n, n)
        return jnp.where(z < n_z - 1 - z, low, n_z - 1 - low)

    def relay(n):
        source_z = nth(n)
        wait_own(source_z)
        sends(source_z, lambda copy: copy.start(), False)

    def relay_other(n):
        source_z = nth(n)

        @pl.when(across_first(source_z, 1))
        def _():
            w_copy(ACROSS, source_z * 2 + 1 - y, 1, False).wait_recv()
            sends_other(source_z, lambda copy: copy.start())

    pick_copies = []
    my_rows = pl.ds(pl.multiple_of(mine * col, mine), mine)
    for step in range(1, n_col):
        copy = remote(
            pbuf.at[:, my_rows], pbuf.at[:, my_rows],
            p_send.at[step], p_recv.at[step], me, lax.rem(col + step, n_col),
        )
        copy.start()
        pick_copies.append(copy)

    relay_other(0)
    relay(1)

    corner_copies = []
    for k in range(k_local):
        coeff_copies[2 * k].wait_recv()
        copy = remote(
            cbuf.at[opposite, k], cbuf.at[opposite, k], c_send.at[2, k], c_recv.at[2, k], me, twin
        )
        copy.start()
        corner_copies.append(copy)
    for copy in pick_copies:
        copy.wait_recv()
    for j in range(2):
        for k in range(k_local):
            turned = pbuf[j * k_local + k].astype(jnp.float32).T.astype(jnp.bfloat16)
            xbuf[k, vectors * j : vectors * (j + 1), :] = turned
    proj[...] = jnp.zeros_like(proj)
    bacc[...] = jnp.zeros_like(bacc)
    for k in range(k_local):
        coeff_copies[2 * k + 1].wait_recv()
        corner_copies[k].wait_recv()

    relay(2)
    relay_other(1)
    relay_other(2)

    def coeff_rows(r, k):
        at = pl.ds(pl.multiple_of(rows * lax.rem(r, 2), rows), rows)
        return cbuf[lax.div(r, 2), k, at, :]

    @pl.loop(0, n_ka)
    def _(r):
        for k in range(k_local):
            both = nt(xbuf[k], coeff_rows(r, k)).astype(jnp.bfloat16)
            for j in range(2):
                dens[j, r, vectors * k : vectors * (k + 1), :] = both[vectors * j : vectors * (j + 1)]

    def project(part, r):
        low = part.astype(jnp.bfloat16)
        for k in range(k_local):
            proj[k] += nn(low[vectors * k : vectors * (k + 1)], coeff_rows(r, k))

    order = (0, 1, 0, 2, 1, 3, 2, 3)
    across = (0, 0, 1, 0, 1, 0, 1, 1)

    @pl.loop(0, n_ka)
    def _(i):
        @pl.when(i == 5)
        def _():
            relay(3)
            relay_other(3)

        source_z = nth(listed(i, order))
        other = listed(i, across)
        source = source_z * 2 + jnp.where(other == 1, 1 - y, y)

        @pl.when(other == 1)
        def _():
            wait_other(source_z)

        half = half_of(source)
        b = 2 * col + half
        part = nt(dens[0, b], wbuf[source, 0]) + nt(dens[1, b], wbuf[source, 1])

        @pl.when(source_z == col)
        def _():
            bacc[half] += part

        @pl.when(source_z != col)
        def _():
            project(part, source)
            bacc[half] += nn(dens[0, source], wbuf[source, 0]) + nn(dens[1, source], wbuf[source, 1])

    bacc[0] += nt(dens[0, 2 * col + 1], ebuf[0]) + nn(dens[1, 2 * col + 1], ebuf[1])
    bacc[1] += nn(dens[0, 2 * col], ebuf[0]) + nt(dens[1, 2 * col], ebuf[1])
    for half in range(2):
        project(bacc[half], 2 * col + half)

    for k in range(k_local):
        turned = proj[k].T.astype(jnp.bfloat16)
        for c in range(n_col):
            outgoing[c, k] = turned[mine * c : mine * (c + 1)]
    out_copies = []
    for step in range(1, n_col):
        to = lax.rem(col + step, n_col)
        copy = remote(
            outgoing.at[to], incoming.at[step], o_send.at[step], o_recv.at[step], me, to
        )
        copy.start()
        out_copies.append(copy)
    total = outgoing[col].astype(jnp.float32)
    for step, copy in enumerate(out_copies, 1):
        copy.wait_recv()
        total += incoming[step].astype(jnp.float32)
    out[...] = total

    for copy in amp_copies + coeff_copies + pick_copies + corner_copies + out_copies:
        copy.wait_send()
    sends(z, lambda copy: copy.wait_send(), True)
    for n in range(1, n_z):
        sends(nth(n), lambda copy: copy.wait_send(), False)
    for source_z in (0, n_z - 1):
        sends_other(source_z, lambda copy: copy.wait_send())


def pick(qsel, w_screen, out, sem):
    copies = [
        pltpu.make_async_copy(w_screen.at[qsel[j]], out.at[j], sem.at[j]) for j in range(2)
    ]
    for copy in copies:
        copy.start()
    for copy in copies:
        copy.wait()


def body(n_ka, n_col, amps, isdf_coeffs, w_screen, energies, qsel, partner):
    k_local, mine, vectors = amps.shape
    pairs = isdf_coeffs.shape[2]
    rows, width = w_screen.shape[1:]
    vmem = pl.BlockSpec(memory_space=pltpu.VMEM)
    dma = pltpu.SemaphoreType.DMA
    bf16, f32 = jnp.bfloat16, jnp.float32
    slabs = pl.pallas_call(
        pick,
        out_shape=jax.ShapeDtypeStruct((2, rows, width), w_screen.dtype),
        in_specs=[pl.BlockSpec(memory_space=pltpu.SMEM), pl.BlockSpec(memory_space=pltpu.HBM)],
        out_specs=vmem,
        scratch_shapes=[dma((2,))],
    )(qsel, w_screen)
    summed = pl.pallas_call(
        functools.partial(kernel, n_ka, n_col),
        out_shape=jax.ShapeDtypeStruct(amps.shape, f32),
        in_specs=[pl.BlockSpec(memory_space=pltpu.SMEM)]
        + [pl.BlockSpec(memory_space=pl.ANY)] * 3,
        out_specs=vmem,
        scratch_shapes=[
            pltpu.VMEM((n_ka * k_local, mine, vectors), bf16),
            pltpu.VMEM((2 * k_local, pairs, vectors), bf16),
            pltpu.VMEM((n_col, k_local, width, pairs), bf16),
            pltpu.VMEM((n_ka, 2, rows, rows), bf16),
            pltpu.VMEM((2, rows, rows), bf16),
            pltpu.VMEM((k_local, 2 * vectors, pairs), bf16),
            pltpu.VMEM((2, n_ka, k_local * vectors, rows), bf16),
            pltpu.VMEM((2, k_local * vectors, rows), f32),
            pltpu.VMEM((k_local, vectors, pairs), f32),
            pltpu.VMEM((n_col, k_local, mine, vectors), bf16),
            pltpu.VMEM((n_col, k_local, mine, vectors), bf16),
            dma((n_ka,)), dma((n_ka,)),
            dma((n_col,)), dma((n_col,)),
            dma((3, k_local)), dma((3, k_local)),
            dma((n_ka, 2, 3)), dma((n_ka, 2)),
            dma((2, 3)), dma((2,)),
            dma((n_col,)), dma((n_col,)),
            dma((5,)),
        ],
        compiler_params=pltpu.CompilerParams(
            collective_id=0, has_side_effects=True, vmem_limit_bytes=48 * 2**20
        ),
    )(partner, amps, isdf_coeffs, slabs)
    return summed + energies[:, :, None] * amps.astype(f32)


def solution(mesh):
    placed = (
        P("ka", "col", None),
        P("ka", "col", None),
        P(None, "ka", "col"),
        P("ka", "col"),
        P(),
        P(),
    )
    n_ka, n_col = mesh.shape["ka"], mesh.shape["col"]
    paired = n_ka == 2 * n_col and n_col == 4
    chosen = functools.partial(body, n_ka, n_col) if paired else general_body
    return jax.shard_map(
        chosen, mesh=mesh, in_specs=placed, out_specs=P("ka", "col", None), check_vma=False
    )
```

```python
import functools

import jax
import jax.numpy as jnp
from jax import lax
from jax.experimental import pallas as pl
from jax.experimental.pallas import tpu as pltpu
from jax.sharding import PartitionSpec as P

MESH = pl.DeviceIdType.MESH
ACROSS, UP, DOWN, UP2, DOWN2 = range(5)


def general_body(amps, isdf_coeffs, w_screen, energies, qsel, partner):
    k_local = amps.shape[0]
    vectors = amps.shape[2]
    offset_base = lax.axis_index("ka") * k_local
    owned = offset_base + jnp.arange(k_local, dtype=jnp.int32)
    wanted = jnp.take(partner, owned, axis=1).reshape(-1)
    everyone = lax.all_gather(amps, "ka", axis=0, tiled=True)
    picked = jnp.take(everyone, wanted, axis=0)
    partners = lax.all_gather(picked, "col", axis=1, tiled=True)
    partners = partners.reshape(2, k_local, partners.shape[1], vectors)
    densities = jnp.einsum(
        "kms,qkse->qmke", isdf_coeffs, partners, preferred_element_type=jnp.float32
    )
    width = densities.shape[1]
    densities = densities.astype(jnp.bfloat16).reshape(2, width, k_local * vectors)
    slabs = jnp.take(w_screen, qsel, axis=0)
    partials = jnp.einsum(
        "qrm,qmx->qrx",
        lax.all_gather(slabs, "ka", axis=1, tiled=True),
        densities,
        preferred_element_type=jnp.float32,
    )
    screened = lax.psum_scatter(
        partials.astype(jnp.bfloat16), "col", scatter_dimension=1, tiled=True
    ).astype(jnp.float32)
    screened = screened.astype(jnp.bfloat16).reshape(2, width, k_local, vectors)
    projected = jnp.einsum(
        "kms,qmke->kse", isdf_coeffs, screened, preferred_element_type=jnp.float32
    )
    summed = lax.psum_scatter(
        projected.astype(jnp.bfloat16), "col", scatter_dimension=1, tiled=True
    ).astype(jnp.float32)
    return summed + energies[:, :, None] * amps.astype(jnp.float32)


def listed(i, values):
    out = jnp.int32(values[0])
    for at, value in enumerate(values[1:], 1):
        out = jnp.where(i == at, jnp.int32(value), out)
    return out


def nt(a, b):
    return lax.dot_general(a, b, (((1,), (1,)), ((), ())), preferred_element_type=jnp.float32)


def nn(a, b):
    return jnp.dot(a, b, preferred_element_type=jnp.float32)


def kernel(
    n_ka, n_col, partner, amps, coeffs, slabs, out,
    abuf, pbuf, cbuf, wbuf, ebuf, xbuf, dens, bacc, proj, outgoing, incoming,
    a_send, a_recv, p_send, p_recv, c_send, c_recv, w_send, w_recv,
    e_send, e_recv, o_send, o_recv, own_sem,
):
    k_local, mine, vectors = amps.shape
    rows = slabs.shape[1]
    me = lax.axis_index("ka")
    col = lax.axis_index("col")
    n_z = n_ka // 2
    z, y = lax.div(me, 2), lax.rem(me, 2)
    beside = me + 1 - 2 * y
    twin = col + 1 - 2 * lax.rem(col, 2)
    opposite = lax.rem(col + 2, n_col)
    corner = lax.rem(twin + 2, n_col)

    def half_of(a):
        odd = lax.rem(a, 2)
        return jnp.where(a >= 2 * col, odd, 1 - odd)

    def remote(src, dst, send, recv, ka, at):
        return pltpu.make_async_remote_copy(
            src_ref=src, dst_ref=dst, send_sem=send, recv_sem=recv,
            device_id={"ka": ka, "col": at}, device_id_type=MESH,
        )

    barrier = pltpu.get_barrier_semaphore()
    for step in range(1, n_ka):
        pl.semaphore_signal(
            barrier, inc=1, device_id={"ka": lax.rem(me + step, n_ka), "col": col},
            device_id_type=MESH,
        )
    for step in range(1, n_col):
        pl.semaphore_signal(
            barrier, inc=1, device_id={"ka": me, "col": lax.rem(col + step, n_col)},
            device_id_type=MESH,
        )
    pl.semaphore_wait(barrier, n_ka + n_col - 2)

    def amp_copy(source, way, to, own):
        slot = abuf.at[pl.ds(source * k_local, k_local)]
        return remote(
            amps if own else slot, slot, a_send.at[source, way], a_recv.at[source], to, col
        )

    amp_sends = [amp_copy(me, 0, beside, True)]
    for step in range(1, n_z):
        amp_sends.append(amp_copy(me, step, lax.rem(z + step, n_z) * 2 + y, True))
    for copy in amp_sends:
        copy.start()

    def coeff_copy(k, way):
        to = (opposite, twin, twin)[way]
        src = coeffs.at[k] if way < 2 else cbuf.at[opposite, k]
        dst = cbuf.at[col if way < 2 else opposite, k]
        return remote(src, dst, c_send.at[way, k], c_recv.at[way, k], me, to)

    def w_copy(way, source, j, own):
        to = (beside, me + 2, me - 2, me + 4, me - 4)[way]
        if own:
            src = slabs.at[j, :, pl.ds(pl.multiple_of(rows * half_of(me), rows), rows)]
        else:
            src = wbuf.at[source, j]
        return remote(src, wbuf.at[source, j], w_send.at[source, j, way], w_recv.at[source, j], to, col)

    own_extra_src = slabs.at[y, :, pl.ds(pl.multiple_of(rows * (1 - y), rows), rows)]

    def e_copy(way, j, own):
        to = (beside, me + 2, me - 2, me + 4, me - 4)[way]
        src = own_extra_src if own else ebuf.at[j]
        return remote(src, ebuf.at[j], e_send.at[j, way], e_recv.at[j], to, col)

    def across_first(source_z, j):
        return (source_z == 0) | (source_z == n_z - 1) if j == 1 else None

    def when(cond, act):
        if cond is None:
            act()
        else:
            pl.when(cond)(act)

    def along(source_z):
        first, after = source_z == z, source_z == z + 2
        before = source_z == z - 2
        return (
            (UP2, first & (z < n_z - 2)), (DOWN2, first & (z > 1)),
            (UP, (first | before) & (z < n_z - 1)), (DOWN, (first | after) & (z > 0)),
        )

    def sends(source_z, go, own):
        source = source_z * 2 + y
        for j in (1, 0):
            early = across_first(source_z, j)
            over = None if own or early is None else jnp.logical_not(early)
            for way, wanted in ((ACROSS, over),) + along(source_z):
                when(wanted, lambda way=way, j=j: go(w_copy(way, source, j, own)))

        @pl.when(source_z == col)
        def _():
            for way, wanted in ((ACROSS, None),) + along(source_z):
                when(wanted, lambda way=way: go(e_copy(way, y, own)))

    end = (z == 0) | (z == n_z - 1)
    passed = jnp.where(end, z, jnp.where(z < n_z - 1 - z, n_z - 1, 0))

    def sends_other(go):
        source = passed * 2 + 1 - y
        for way, wanted in along(passed):
            when(wanted, lambda way=way: go(w_copy(way, source, 1, False)))

    def relay_other():
        w_copy(ACROSS, passed * 2 + 1 - y, 1, False).wait_recv()
        sends_other(lambda copy: copy.start())

    def wait_own(source_z):
        source = source_z * 2 + y
        for j in range(2):
            w_copy(ACROSS, source, j, False).wait_recv()
        pl.when(source_z == col)(lambda: e_copy(ACROSS, y, False).wait_recv())

    def wait_other(source_z):
        source = source_z * 2 + 1 - y
        w_copy(ACROSS, source, 0, False).wait_recv()
        pl.when(source_z != passed)(
            lambda: w_copy(ACROSS, source, 1, False).wait_recv()
        )
        pl.when(source_z == col)(lambda: e_copy(ACROSS, 1 - y, False).wait_recv())

    sends(z, lambda copy: copy.start(), True)

    for way in range(2):
        coeff_copy(0, way).start()

    local = [
        pltpu.make_async_copy(amps, abuf.at[pl.ds(me * k_local, k_local)], own_sem.at[0]),
        pltpu.make_async_copy(coeffs, cbuf.at[col], own_sem.at[1]),
    ]
    for j in range(2):
        local.append(
            pltpu.make_async_copy(
                slabs.at[j, :, pl.ds(pl.multiple_of(rows * half_of(me), rows), rows)],
                wbuf.at[me, j], own_sem.at[2 + j],
            )
        )
    for copy in local:
        copy.start()

    @pl.when(z == col)
    def _():
        copy = pltpu.make_async_copy(own_extra_src, ebuf.at[y], own_sem.at[4])
        copy.start()
        copy.wait()

    for copy in local:
        copy.wait()
    for step in range(1, n_z):
        source = lax.rem(z + step, n_z) * 2 + y
        copy = amp_copy(source, 0, beside, False)
        copy.wait_recv()
        copy.start()
        amp_sends.append(copy)
    for step in range(n_z):
        amp_copy(lax.rem(z + step, n_z) * 2 + 1 - y, 0, beside, False).wait_recv()

    for j in range(2):
        for k in range(k_local):
            at = partner[j, me * k_local + k]
            pbuf[j * k_local + k, pl.ds(pl.multiple_of(mine * col, mine), mine), :] = abuf[at]

    my_rows = pl.ds(pl.multiple_of(mine * col, mine), mine)
    far_rows = pl.ds(pl.multiple_of(mine * opposite, mine), mine)

    def pick_copy(way):
        rows_of = my_rows if way < 2 else far_rows
        return remote(
            pbuf.at[:, rows_of], pbuf.at[:, rows_of],
            p_send.at[way], p_recv.at[way], me, (opposite, twin, twin)[way],
        )

    for way in range(2):
        pick_copy(way).start()
    for k in range(1, k_local):
        for way in range(2):
            coeff_copy(k, way).start()

    def nth(n):
        low = z < n_z - 1 - z
        near = jnp.where(low, z, n_z - 1 - z)
        turn = jnp.where(near == 0, n, jnp.where(n == 0, near, jnp.where(n == 1, n_z - 1, 2 * (n - 2))))
        return jnp.where(low, turn, n_z - 1 - turn)

    def relay(n):
        source_z = nth(n)
        wait_own(source_z)
        sends(source_z, lambda copy: copy.start(), False)

    pl.when(end)(relay_other)
    relay(1)

    coeff_copy(0, 0).wait_recv()
    coeff_copy(0, 2).start()
    pick_copy(0).wait_recv()
    pick_copy(2).start()
    relay(2)
    for k in range(1, k_local):
        coeff_copy(k, 0).wait_recv()
        coeff_copy(k, 2).start()
    pl.when(jnp.logical_not(end))(relay_other)
    for way in (1, 2):
        pick_copy(way).wait_recv()
    for j in range(2):
        for k in range(k_local):
            turned = pbuf[j * k_local + k].astype(jnp.float32).T.astype(jnp.bfloat16)
            xbuf[k, vectors * j : vectors * (j + 1), :] = turned
    proj[...] = jnp.zeros_like(proj)
    bacc[...] = jnp.zeros_like(bacc)
    for k in range(k_local):
        for way in (1, 2):
            coeff_copy(k, way).wait_recv()

    def coeff_rows(r, k):
        at = pl.ds(pl.multiple_of(rows * lax.rem(r, 2), rows), rows)
        return cbuf[lax.div(r, 2), k, at, :]

    @pl.loop(0, n_ka)
    def _(r):
        for k in range(k_local):
            both = nt(xbuf[k], coeff_rows(r, k)).astype(jnp.bfloat16)
            for j in range(2):
                dens[j, r, vectors * k : vectors * (k + 1), :] = both[vectors * j : vectors * (j + 1)]

    def project(part, r):
        low = part.astype(jnp.bfloat16)
        for k in range(k_local):
            proj[k] += nn(low[vectors * k : vectors * (k + 1)], coeff_rows(r, k))

    order = (0, 1, 0, 2, 1, 3, 2, 3)
    across = (0, 0, 1, 0, 1, 0, 1, 1)

    @pl.loop(0, n_ka)
    def _(i):
        @pl.when(i == 5)
        def _():
            relay(3)

        source_z = nth(listed(i, order))
        other = listed(i, across)
        source = source_z * 2 + jnp.where(other == 1, 1 - y, y)

        @pl.when(other == 1)
        def _():
            wait_other(source_z)

        half = half_of(source)
        b = 2 * col + half
        part = nt(dens[0, b], wbuf[source, 0]) + nt(dens[1, b], wbuf[source, 1])

        @pl.when(source_z == col)
        def _():
            bacc[half] += part

        @pl.when(source_z != col)
        def _():
            project(part, source)
            bacc[half] += nn(dens[0, source], wbuf[source, 0]) + nn(dens[1, source], wbuf[source, 1])

    bacc[0] += nt(dens[0, 2 * col + 1], ebuf[0]) + nn(dens[1, 2 * col + 1], ebuf[1])
    bacc[1] += nn(dens[0, 2 * col], ebuf[0]) + nt(dens[1, 2 * col], ebuf[1])
    for half in range(2):
        project(bacc[half], 2 * col + half)

    for k in range(k_local):
        turned = proj[k].T.astype(jnp.bfloat16)
        for c in range(n_col):
            outgoing[c, k] = turned[mine * c : mine * (c + 1)]
    out_copies = []
    for step in range(1, n_col):
        to = lax.rem(col + step, n_col)
        copy = remote(
            outgoing.at[to], incoming.at[step], o_send.at[step], o_recv.at[step], me, to
        )
        copy.start()
        out_copies.append(copy)
    total = outgoing[col].astype(jnp.float32)
    for step, copy in enumerate(out_copies, 1):
        copy.wait_recv()
        total += incoming[step].astype(jnp.float32)
    out[...] = total

    for copy in amp_sends + out_copies:
        copy.wait_send()
    for way in range(3):
        pick_copy(way).wait_send()
        for k in range(k_local):
            coeff_copy(k, way).wait_send()
    sends(z, lambda copy: copy.wait_send(), True)
    for n in range(1, n_z):
        sends(nth(n), lambda copy: copy.wait_send(), False)
    sends_other(lambda copy: copy.wait_send())


def pick(qsel, w_screen, out, sem):
    copies = [
        pltpu.make_async_copy(w_screen.at[qsel[j]], out.at[j], sem.at[j]) for j in range(2)
    ]
    for copy in copies:
        copy.start()
    for copy in copies:
        copy.wait()


def body(n_ka, n_col, amps, isdf_coeffs, w_screen, energies, qsel, partner):
    k_local, mine, vectors = amps.shape
    pairs = isdf_coeffs.shape[2]
    rows, width = w_screen.shape[1:]
    vmem = pl.BlockSpec(memory_space=pltpu.VMEM)
    dma = pltpu.SemaphoreType.DMA
    bf16, f32 = jnp.bfloat16, jnp.float32
    slabs = pl.pallas_call(
        pick,
        out_shape=jax.ShapeDtypeStruct((2, rows, width), w_screen.dtype),
        in_specs=[pl.BlockSpec(memory_space=pltpu.SMEM), pl.BlockSpec(memory_space=pltpu.HBM)],
        out_specs=vmem,
        scratch_shapes=[dma((2,))],
    )(qsel, w_screen)
    summed = pl.pallas_call(
        functools.partial(kernel, n_ka, n_col),
        out_shape=jax.ShapeDtypeStruct(amps.shape, f32),
        in_specs=[pl.BlockSpec(memory_space=pltpu.SMEM)]
        + [pl.BlockSpec(memory_space=pl.ANY)] * 3,
        out_specs=vmem,
        scratch_shapes=[
            pltpu.VMEM((n_ka * k_local, mine, vectors), bf16),
            pltpu.VMEM((2 * k_local, pairs, vectors), bf16),
            pltpu.VMEM((n_col, k_local, width, pairs), bf16),
            pltpu.VMEM((n_ka, 2, rows, rows), bf16),
            pltpu.VMEM((2, rows, rows), bf16),
            pltpu.VMEM((k_local, 2 * vectors, pairs), bf16),
            pltpu.VMEM((2, n_ka, k_local * vectors, rows), bf16),
            pltpu.VMEM((2, k_local * vectors, rows), f32),
            pltpu.VMEM((k_local, vectors, pairs), f32),
            pltpu.VMEM((n_col, k_local, mine, vectors), bf16),
            pltpu.VMEM((n_col, k_local, mine, vectors), bf16),
            dma((n_ka, n_ka // 2)), dma((n_ka,)),
            dma((3,)), dma((3,)),
            dma((3, k_local)), dma((3, k_local)),
            dma((n_ka, 2, 5)), dma((n_ka, 2)),
            dma((2, 5)), dma((2,)),
            dma((n_col,)), dma((n_col,)),
            dma((5,)),
        ],
        compiler_params=pltpu.CompilerParams(
            collective_id=0, has_side_effects=True, vmem_limit_bytes=48 * 2**20
        ),
    )(partner, amps, isdf_coeffs, slabs)
    return summed + energies[:, :, None] * amps.astype(f32)


def solution(mesh):
    placed = (
        P("ka", "col", None),
        P("ka", "col", None),
        P(None, "ka", "col"),
        P("ka", "col"),
        P(),
        P(),
    )
    n_ka, n_col = mesh.shape["ka"], mesh.shape["col"]
    paired = n_ka == 2 * n_col and n_col == 4
    chosen = functools.partial(body, n_ka, n_col) if paired else general_body
    return jax.shard_map(
        chosen, mesh=mesh, in_specs=placed, out_specs=P("ka", "col", None), check_vma=False
    )
```

```python
import functools

import jax
import jax.numpy as jnp
from jax import lax
from jax.experimental import pallas as pl
from jax.experimental.pallas import tpu as pltpu
from jax.sharding import PartitionSpec as P

MESH = pl.DeviceIdType.MESH
ACROSS, UP, DOWN, UP2, DOWN2 = range(5)


def general_body(amps, isdf_coeffs, w_screen, energies, qsel, partner):
    k_local = amps.shape[0]
    vectors = amps.shape[2]
    offset_base = lax.axis_index("ka") * k_local
    owned = offset_base + jnp.arange(k_local, dtype=jnp.int32)
    wanted = jnp.take(partner, owned, axis=1).reshape(-1)
    everyone = lax.all_gather(amps, "ka", axis=0, tiled=True)
    picked = jnp.take(everyone, wanted, axis=0)
    partners = lax.all_gather(picked, "col", axis=1, tiled=True)
    partners = partners.reshape(2, k_local, partners.shape[1], vectors)
    densities = jnp.einsum(
        "kms,qkse->qmke", isdf_coeffs, partners, preferred_element_type=jnp.float32
    )
    width = densities.shape[1]
    densities = densities.astype(jnp.bfloat16).reshape(2, width, k_local * vectors)
    slabs = jnp.take(w_screen, qsel, axis=0)
    partials = jnp.einsum(
        "qrm,qmx->qrx",
        lax.all_gather(slabs, "ka", axis=1, tiled=True),
        densities,
        preferred_element_type=jnp.float32,
    )
    screened = lax.psum_scatter(
        partials.astype(jnp.bfloat16), "col", scatter_dimension=1, tiled=True
    ).astype(jnp.float32)
    screened = screened.astype(jnp.bfloat16).reshape(2, width, k_local, vectors)
    projected = jnp.einsum(
        "kms,qmke->kse", isdf_coeffs, screened, preferred_element_type=jnp.float32
    )
    summed = lax.psum_scatter(
        projected.astype(jnp.bfloat16), "col", scatter_dimension=1, tiled=True
    ).astype(jnp.float32)
    return summed + energies[:, :, None] * amps.astype(jnp.float32)


def listed(i, values):
    out = jnp.int32(values[0])
    for at, value in enumerate(values[1:], 1):
        out = jnp.where(i == at, jnp.int32(value), out)
    return out


def nt(a, b):
    return lax.dot_general(a, b, (((1,), (1,)), ((), ())), preferred_element_type=jnp.float32)


def nn(a, b):
    return jnp.dot(a, b, preferred_element_type=jnp.float32)


def kernel(
    n_ka, n_col, partner, amps, coeffs, slabs, out,
    abuf, pbuf, cbuf, wbuf, ebuf, xbuf, dens, bacc, proj, outgoing, incoming,
    a_send, a_recv, p_send, p_recv, c_send, c_recv, w_send, w_recv,
    e_send, e_recv, o_send, o_recv, own_sem,
):
    k_local, mine, vectors = amps.shape
    rows = slabs.shape[1]
    me = lax.axis_index("ka")
    col = lax.axis_index("col")
    n_z = n_ka // 2
    z, y = lax.div(me, 2), lax.rem(me, 2)
    beside = me + 1 - 2 * y
    twin = col + 1 - 2 * lax.rem(col, 2)
    opposite = lax.rem(col + 2, n_col)
    corner = lax.rem(twin + 2, n_col)

    def half_of(a):
        odd = lax.rem(a, 2)
        return jnp.where(a >= 2 * col, odd, 1 - odd)

    def remote(src, dst, send, recv, ka, at):
        return pltpu.make_async_remote_copy(
            src_ref=src, dst_ref=dst, send_sem=send, recv_sem=recv,
            device_id={"ka": ka, "col": at}, device_id_type=MESH,
        )

    barrier = pltpu.get_barrier_semaphore()
    for step in range(1, n_ka):
        pl.semaphore_signal(
            barrier, inc=1, device_id={"ka": lax.rem(me + step, n_ka), "col": col},
            device_id_type=MESH,
        )
    for step in range(1, n_col):
        pl.semaphore_signal(
            barrier, inc=1, device_id={"ka": me, "col": lax.rem(col + step, n_col)},
            device_id_type=MESH,
        )
    pl.semaphore_wait(barrier, n_ka + n_col - 2)

    def amp_copy(source, way, to, own):
        slot = abuf.at[pl.ds(source * k_local, k_local)]
        return remote(
            amps if own else slot, slot, a_send.at[source, way], a_recv.at[source], to, col
        )

    amp_sends = [amp_copy(me, 0, beside, True)]
    for step in range(1, n_z):
        amp_sends.append(amp_copy(me, step, lax.rem(z + step, n_z) * 2 + y, True))
    for copy in amp_sends:
        copy.start()

    def coeff_copy(k, way):
        to = (opposite, twin, twin)[way]
        src = coeffs.at[k] if way < 2 else cbuf.at[opposite, k]
        dst = cbuf.at[col if way < 2 else opposite, k]
        return remote(src, dst, c_send.at[way, k], c_recv.at[way, k], me, to)

    piece_rows = rows // 2

    def w_copy(way, source, u, own):
        to = (beside, me + 2, me - 2, me + 4, me - 4)[way]
        j, at = u // 2, pl.ds(u % 2 * piece_rows, piece_rows)
        dst = wbuf.at[source, j, at]
        if own:
            src = slabs.at[j, at, pl.ds(pl.multiple_of(rows * half_of(me), rows), rows)]
        else:
            src = dst
        return remote(src, dst, w_send.at[source, u, way], w_recv.at[source, u], to, col)

    own_extra_src = slabs.at[y, :, pl.ds(pl.multiple_of(rows * (1 - y), rows), rows)]

    def e_copy(way, j, own):
        to = (beside, me + 2, me - 2, me + 4, me - 4)[way]
        src = own_extra_src if own else ebuf.at[j]
        return remote(src, ebuf.at[j], e_send.at[j, way], e_recv.at[j], to, col)

    def across_first(source_z, j):
        return (source_z == 0) | (source_z == n_z - 1) if j == 1 else None

    def when(cond, act):
        if cond is None:
            act()
        else:
            pl.when(cond)(act)

    def along(source_z):
        first, after = source_z == z, source_z == z + 2
        before = source_z == z - 2
        return (
            (UP2, first & (z < n_z - 2)), (DOWN2, first & (z > 1)),
            (UP, (first | before) & (z < n_z - 1)), (DOWN, (first | after) & (z > 0)),
        )

    def send_piece(source_z, u, go, own, ways=range(5)):
        early = across_first(source_z, u // 2)
        over = None if own or early is None else jnp.logical_not(early)
        for way, wanted in ((ACROSS, over),) + along(source_z):
            if way in ways:
                when(wanted, lambda way=way: go(w_copy(way, source_z * 2 + y, u, own)))

    def send_extra(source_z, go, own):
        @pl.when(source_z == col)
        def _():
            for way, wanted in ((ACROSS, None),) + along(source_z):
                when(wanted, lambda way=way: go(e_copy(way, y, own)))

    def sends(source_z, go, own):
        for u in (2, 3, 0, 1):
            send_piece(source_z, u, go, own)
        send_extra(source_z, go, own)

    end = (z == 0) | (z == n_z - 1)
    passed = jnp.where(end, z, jnp.where(z < n_z - 1 - z, n_z - 1, 0))

    def sends_other(go):
        source = passed * 2 + 1 - y
        for u in (2, 3):
            for way, wanted in along(passed):
                when(wanted, lambda way=way, u=u: go(w_copy(way, source, u, False)))

    def relay_other():
        source = passed * 2 + 1 - y
        for u in (2, 3):
            w_copy(ACROSS, source, u, False).wait_recv()
            for way, wanted in along(passed):
                when(wanted, lambda way=way, u=u: w_copy(way, source, u, False).start())

    def wait_other(source_z):
        source = source_z * 2 + 1 - y
        for u in (0, 1):
            w_copy(ACROSS, source, u, False).wait_recv()

        @pl.when(source_z != passed)
        def _():
            for u in (2, 3):
                w_copy(ACROSS, source, u, False).wait_recv()

        pl.when(source_z == col)(lambda: e_copy(ACROSS, 1 - y, False).wait_recv())

    start = lambda copy: copy.start()
    for u in (2, 3):
        send_piece(z, u, start, True)
    for k in range(k_local):
        for way in range(2):
            coeff_copy(k, way).start()
    for u in (0, 1):
        send_piece(z, u, start, True, (UP, DOWN, UP2, DOWN2))

    local = [
        pltpu.make_async_copy(amps, abuf.at[pl.ds(me * k_local, k_local)], own_sem.at[0]),
        pltpu.make_async_copy(coeffs, cbuf.at[col], own_sem.at[1]),
    ]
    for j in range(2):
        local.append(
            pltpu.make_async_copy(
                slabs.at[j, :, pl.ds(pl.multiple_of(rows * half_of(me), rows), rows)],
                wbuf.at[me, j], own_sem.at[2 + j],
            )
        )
    for copy in local:
        copy.start()

    @pl.when(z == col)
    def _():
        copy = pltpu.make_async_copy(own_extra_src, ebuf.at[y], own_sem.at[4])
        copy.start()
        copy.wait()

    for copy in local:
        copy.wait()
    for step in range(1, n_z):
        source = lax.rem(z + step, n_z) * 2 + y
        copy = amp_copy(source, 0, beside, False)
        copy.wait_recv()
        copy.start()
        amp_sends.append(copy)
    for u in (0, 1):
        send_piece(z, u, start, True, (ACROSS,))
    send_extra(z, start, True)
    pl.when(end)(relay_other)

    def nth(n):
        low = z < n_z - 1 - z
        near = jnp.where(low, z, n_z - 1 - z)
        turn = jnp.where(near == 0, n, jnp.where(n == 0, near, jnp.where(n == 1, n_z - 1, 2 * (n - 2))))
        return jnp.where(low, turn, n_z - 1 - turn)

    def relay(n):
        source_z = nth(n)
        for u in (2, 3, 0, 1):
            w_copy(ACROSS, source_z * 2 + y, u, False).wait_recv()
            send_piece(source_z, u, start, False)
        pl.when(source_z == col)(lambda: e_copy(ACROSS, y, False).wait_recv())
        send_extra(source_z, start, False)

    for step in range(n_z):
        amp_copy(lax.rem(z + step, n_z) * 2 + 1 - y, 0, beside, False).wait_recv()

    for j in range(2):
        for k in range(k_local):
            at = partner[j, me * k_local + k]
            pbuf[j * k_local + k, pl.ds(pl.multiple_of(mine * col, mine), mine), :] = abuf[at]

    my_rows = pl.ds(pl.multiple_of(mine * col, mine), mine)
    far_rows = pl.ds(pl.multiple_of(mine * opposite, mine), mine)

    def pick_copy(way):
        rows_of = my_rows if way < 2 else far_rows
        return remote(
            pbuf.at[:, rows_of], pbuf.at[:, rows_of],
            p_send.at[way], p_recv.at[way], me, (opposite, twin, twin)[way],
        )

    for way in range(2):
        pick_copy(way).start()

    for k in range(k_local):
        coeff_copy(k, 0).wait_recv()
        coeff_copy(k, 2).start()
    relay(1)
    pick_copy(0).wait_recv()
    pick_copy(2).start()
    for way in (1, 2):
        pick_copy(way).wait_recv()
    for j in range(2):
        for k in range(k_local):
            turned = pbuf[j * k_local + k].astype(jnp.float32).T.astype(jnp.bfloat16)
            xbuf[k, vectors * j : vectors * (j + 1), :] = turned
    proj[...] = jnp.zeros_like(proj)
    bacc[...] = jnp.zeros_like(bacc)
    for k in range(k_local):
        for way in (1, 2):
            coeff_copy(k, way).wait_recv()

    def coeff_rows(r, k):
        at = pl.ds(pl.multiple_of(rows * lax.rem(r, 2), rows), rows)
        return cbuf[lax.div(r, 2), k, at, :]

    @pl.loop(0, n_ka)
    def _(r):
        for k in range(k_local):
            both = nt(xbuf[k], coeff_rows(r, k)).astype(jnp.bfloat16)
            for j in range(2):
                dens[j, r, vectors * k : vectors * (k + 1), :] = both[vectors * j : vectors * (j + 1)]

    pl.when(jnp.logical_not(end))(relay_other)
    relay(2)

    def project(part, r):
        low = part.astype(jnp.bfloat16)
        for k in range(k_local):
            proj[k] += nn(low[vectors * k : vectors * (k + 1)], coeff_rows(r, k))

    order = (0, 1, 0, 2, 1, 3, 2, 3)
    across = (0, 0, 1, 0, 1, 0, 1, 1)

    @pl.loop(0, n_ka)
    def _(i):
        @pl.when(i == 5)
        def _():
            relay(3)

        source_z = nth(listed(i, order))
        other = listed(i, across)
        source = source_z * 2 + jnp.where(other == 1, 1 - y, y)

        @pl.when(other == 1)
        def _():
            wait_other(source_z)

        half = half_of(source)
        b = 2 * col + half
        part = nt(dens[0, b], wbuf[source, 0]) + nt(dens[1, b], wbuf[source, 1])

        @pl.when(source_z == col)
        def _():
            bacc[half] += part

        @pl.when(source_z != col)
        def _():
            project(part, source)
            bacc[half] += nn(dens[0, source], wbuf[source, 0]) + nn(dens[1, source], wbuf[source, 1])

    bacc[0] += nt(dens[0, 2 * col + 1], ebuf[0]) + nn(dens[1, 2 * col + 1], ebuf[1])
    bacc[1] += nn(dens[0, 2 * col], ebuf[0]) + nt(dens[1, 2 * col], ebuf[1])
    for half in range(2):
        project(bacc[half], 2 * col + half)

    for k in range(k_local):
        turned = proj[k].T.astype(jnp.bfloat16)
        for c in range(n_col):
            outgoing[c, k] = turned[mine * c : mine * (c + 1)]
    out_copies = []
    for step in range(1, n_col):
        to = lax.rem(col + step, n_col)
        copy = remote(
            outgoing.at[to], incoming.at[step], o_send.at[step], o_recv.at[step], me, to
        )
        copy.start()
        out_copies.append(copy)
    total = outgoing[col].astype(jnp.float32)
    for step, copy in enumerate(out_copies, 1):
        copy.wait_recv()
        total += incoming[step].astype(jnp.float32)
    out[...] = total

    for copy in amp_sends + out_copies:
        copy.wait_send()
    for way in range(3):
        pick_copy(way).wait_send()
        for k in range(k_local):
            coeff_copy(k, way).wait_send()
    sends(z, lambda copy: copy.wait_send(), True)
    for n in range(1, n_z):
        sends(nth(n), lambda copy: copy.wait_send(), False)
    sends_other(lambda copy: copy.wait_send())


def pick(qsel, w_screen, out, sem):
    copies = [
        pltpu.make_async_copy(w_screen.at[qsel[j]], out.at[j], sem.at[j]) for j in range(2)
    ]
    for copy in copies:
        copy.start()
    for copy in copies:
        copy.wait()


def body(n_ka, n_col, amps, isdf_coeffs, w_screen, energies, qsel, partner):
    k_local, mine, vectors = amps.shape
    pairs = isdf_coeffs.shape[2]
    rows, width = w_screen.shape[1:]
    vmem = pl.BlockSpec(memory_space=pltpu.VMEM)
    dma = pltpu.SemaphoreType.DMA
    bf16, f32 = jnp.bfloat16, jnp.float32
    slabs = pl.pallas_call(
        pick,
        out_shape=jax.ShapeDtypeStruct((2, rows, width), w_screen.dtype),
        in_specs=[pl.BlockSpec(memory_space=pltpu.SMEM), pl.BlockSpec(memory_space=pltpu.HBM)],
        out_specs=vmem,
        scratch_shapes=[dma((2,))],
    )(qsel, w_screen)
    summed = pl.pallas_call(
        functools.partial(kernel, n_ka, n_col),
        out_shape=jax.ShapeDtypeStruct(amps.shape, f32),
        in_specs=[pl.BlockSpec(memory_space=pltpu.SMEM)]
        + [pl.BlockSpec(memory_space=pl.ANY)] * 2
        + [pl.BlockSpec(memory_space=pltpu.HBM)],
        out_specs=vmem,
        scratch_shapes=[
            pltpu.VMEM((n_ka * k_local, mine, vectors), bf16),
            pltpu.VMEM((2 * k_local, pairs, vectors), bf16),
            pltpu.VMEM((n_col, k_local, width, pairs), bf16),
            pltpu.VMEM((n_ka, 2, rows, rows), bf16),
            pltpu.VMEM((2, rows, rows), bf16),
            pltpu.VMEM((k_local, 2 * vectors, pairs), bf16),
            pltpu.VMEM((2, n_ka, k_local * vectors, rows), bf16),
            pltpu.VMEM((2, k_local * vectors, rows), f32),
            pltpu.VMEM((k_local, vectors, pairs), f32),
            pltpu.VMEM((n_col, k_local, mine, vectors), bf16),
            pltpu.VMEM((n_col, k_local, mine, vectors), bf16),
            dma((n_ka, n_ka // 2)), dma((n_ka,)),
            dma((3,)), dma((3,)),
            dma((3, k_local)), dma((3, k_local)),
            dma((n_ka, 4, 5)), dma((n_ka, 4)),
            dma((2, 5)), dma((2,)),
            dma((n_col,)), dma((n_col,)),
            dma((5,)),
        ],
        compiler_params=pltpu.CompilerParams(
            collective_id=0, has_side_effects=True, vmem_limit_bytes=48 * 2**20
        ),
    )(partner, amps, isdf_coeffs, slabs)
    return summed + energies[:, :, None] * amps.astype(f32)


def solution(mesh):
    placed = (
        P("ka", "col", None),
        P("ka", "col", None),
        P(None, "ka", "col"),
        P("ka", "col"),
        P(),
        P(),
    )
    n_ka, n_col = mesh.shape["ka"], mesh.shape["col"]
    paired = n_ka == 2 * n_col and n_col == 4
    chosen = functools.partial(body, n_ka, n_col) if paired else general_body
    return jax.shard_map(
        chosen, mesh=mesh, in_specs=placed, out_specs=P("ka", "col", None), check_vma=False
    )
```

```python
import functools

import jax
import jax.numpy as jnp
from jax import lax
from jax.experimental import pallas as pl
from jax.experimental.pallas import tpu as pltpu
from jax.sharding import PartitionSpec as P

MESH = pl.DeviceIdType.MESH
ACROSS, UP, DOWN, UP2, DOWN2 = range(5)


def general_body(amps, isdf_coeffs, w_screen, energies, qsel, partner):
    k_local = amps.shape[0]
    vectors = amps.shape[2]
    offset_base = lax.axis_index("ka") * k_local
    owned = offset_base + jnp.arange(k_local, dtype=jnp.int32)
    wanted = jnp.take(partner, owned, axis=1).reshape(-1)
    everyone = lax.all_gather(amps, "ka", axis=0, tiled=True)
    picked = jnp.take(everyone, wanted, axis=0)
    partners = lax.all_gather(picked, "col", axis=1, tiled=True)
    partners = partners.reshape(2, k_local, partners.shape[1], vectors)
    densities = jnp.einsum(
        "kms,qkse->qmke", isdf_coeffs, partners, preferred_element_type=jnp.float32
    )
    width = densities.shape[1]
    densities = densities.astype(jnp.bfloat16).reshape(2, width, k_local * vectors)
    slabs = jnp.take(w_screen, qsel, axis=0)
    partials = jnp.einsum(
        "qrm,qmx->qrx",
        lax.all_gather(slabs, "ka", axis=1, tiled=True),
        densities,
        preferred_element_type=jnp.float32,
    )
    screened = lax.psum_scatter(
        partials.astype(jnp.bfloat16), "col", scatter_dimension=1, tiled=True
    ).astype(jnp.float32)
    screened = screened.astype(jnp.bfloat16).reshape(2, width, k_local, vectors)
    projected = jnp.einsum(
        "kms,qmke->kse", isdf_coeffs, screened, preferred_element_type=jnp.float32
    )
    summed = lax.psum_scatter(
        projected.astype(jnp.bfloat16), "col", scatter_dimension=1, tiled=True
    ).astype(jnp.float32)
    return summed + energies[:, :, None] * amps.astype(jnp.float32)


def listed(i, values):
    out = jnp.int32(values[0])
    for at, value in enumerate(values[1:], 1):
        out = jnp.where(i == at, jnp.int32(value), out)
    return out


def nt(a, b):
    return lax.dot_general(a, b, (((1,), (1,)), ((), ())), preferred_element_type=jnp.float32)


def nn(a, b):
    return jnp.dot(a, b, preferred_element_type=jnp.float32)


def kernel(
    n_ka, n_col, partner, amps, coeffs, slabs, out,
    abuf, pbuf, cbuf, wbuf, ebuf, xbuf, dens, bacc, proj, outgoing, incoming,
    a_send, a_recv, p_send, p_recv, c_send, c_recv, w_send, w_recv,
    e_send, e_recv, o_send, o_recv, own_sem,
):
    k_local, mine, vectors = amps.shape
    rows = slabs.shape[1]
    me = lax.axis_index("ka")
    col = lax.axis_index("col")
    n_z = n_ka // 2
    z, y = lax.div(me, 2), lax.rem(me, 2)
    beside = me + 1 - 2 * y
    twin = col + 1 - 2 * lax.rem(col, 2)
    opposite = lax.rem(col + 2, n_col)
    corner = lax.rem(twin + 2, n_col)

    def half_of(a):
        odd = lax.rem(a, 2)
        return jnp.where(a >= 2 * col, odd, 1 - odd)

    def remote(src, dst, send, recv, ka, at):
        return pltpu.make_async_remote_copy(
            src_ref=src, dst_ref=dst, send_sem=send, recv_sem=recv,
            device_id={"ka": ka, "col": at}, device_id_type=MESH,
        )

    barrier = pltpu.get_barrier_semaphore()
    for step in range(1, n_ka):
        pl.semaphore_signal(
            barrier, inc=1, device_id={"ka": lax.rem(me + step, n_ka), "col": col},
            device_id_type=MESH,
        )
    for step in range(1, n_col):
        pl.semaphore_signal(
            barrier, inc=1, device_id={"ka": me, "col": lax.rem(col + step, n_col)},
            device_id_type=MESH,
        )
    pl.semaphore_wait(barrier, n_ka + n_col - 2)

    def amp_copy(source, way, to, own):
        slot = abuf.at[pl.ds(source * k_local, k_local)]
        return remote(
            amps if own else slot, slot, a_send.at[source, way], a_recv.at[source], to, col
        )

    amp_sends = [amp_copy(me, 0, beside, True)]
    for step in range(1, n_z):
        amp_sends.append(amp_copy(me, step, lax.rem(z + step, n_z) * 2 + y, True))
    for copy in amp_sends:
        copy.start()

    def coeff_copy(k, way):
        to = (opposite, twin, twin)[way]
        src = coeffs.at[k] if way < 2 else cbuf.at[opposite, k]
        dst = cbuf.at[col if way < 2 else opposite, k]
        return remote(src, dst, c_send.at[way, k], c_recv.at[way, k], me, to)

    piece_rows = rows // 2

    def w_copy(way, source, u, own):
        to = (beside, me + 2, me - 2, me + 4, me - 4)[way]
        j, at = u // 2, pl.ds(u % 2 * piece_rows, piece_rows)
        dst = wbuf.at[source, j, at]
        if own:
            src = slabs.at[j, at, pl.ds(pl.multiple_of(rows * half_of(me), rows), rows)]
        else:
            src = dst
        return remote(src, dst, w_send.at[source, u, way], w_recv.at[source, u], to, col)

    own_extra_src = slabs.at[y, :, pl.ds(pl.multiple_of(rows * (1 - y), rows), rows)]

    def e_copy(way, j, own):
        to = (beside, me + 2, me - 2, me + 4, me - 4)[way]
        src = own_extra_src if own else ebuf.at[j]
        return remote(src, ebuf.at[j], e_send.at[j, way], e_recv.at[j], to, col)

    def across_first(source_z, j):
        return (source_z == 0) | (source_z == n_z - 1) if j == 1 else None

    def when(cond, act):
        if cond is None:
            act()
        else:
            pl.when(cond)(act)

    def along(source_z):
        first, after = source_z == z, source_z == z + 2
        before = source_z == z - 2
        return (
            (UP2, first & (z < n_z - 2)), (DOWN2, first & (z > 1)),
            (UP, (first | before) & (z < n_z - 1)), (DOWN, (first | after) & (z > 0)),
        )

    def send_piece(source_z, u, go, own, ways=range(5)):
        early = across_first(source_z, u // 2)
        over = None if own or early is None else jnp.logical_not(early)
        for way, wanted in ((ACROSS, over),) + along(source_z):
            if way in ways:
                when(wanted, lambda way=way: go(w_copy(way, source_z * 2 + y, u, own)))

    def send_extra(source_z, go, own):
        @pl.when(source_z == col)
        def _():
            for way, wanted in ((ACROSS, None),) + along(source_z):
                when(wanted, lambda way=way: go(e_copy(way, y, own)))

    def sends(source_z, go, own):
        for u in (2, 3, 0, 1):
            send_piece(source_z, u, go, own)
        send_extra(source_z, go, own)

    end = (z == 0) | (z == n_z - 1)
    passed = jnp.where(end, z, jnp.where(z < n_z - 1 - z, n_z - 1, 0))

    def sends_other(go):
        source = passed * 2 + 1 - y
        for u in (2, 3):
            for way, wanted in along(passed):
                when(wanted, lambda way=way, u=u: go(w_copy(way, source, u, False)))

    def relay_other():
        source = passed * 2 + 1 - y
        for u in (2, 3):
            w_copy(ACROSS, source, u, False).wait_recv()
            for way, wanted in along(passed):
                when(wanted, lambda way=way, u=u: w_copy(way, source, u, False).start())

    def wait_other(source_z):
        source = source_z * 2 + 1 - y
        for u in (0, 1):
            w_copy(ACROSS, source, u, False).wait_recv()

        @pl.when(source_z != passed)
        def _():
            for u in (2, 3):
                w_copy(ACROSS, source, u, False).wait_recv()

        pl.when(source_z == col)(lambda: e_copy(ACROSS, 1 - y, False).wait_recv())

    start = lambda copy: copy.start()
    for u in (2, 3):
        send_piece(z, u, start, True)
    for k in range(k_local):
        for way in range(2):
            coeff_copy(k, way).start()
    for u in (0, 1):
        send_piece(z, u, start, True, (UP, DOWN, UP2, DOWN2))

    local = [
        pltpu.make_async_copy(amps, abuf.at[pl.ds(me * k_local, k_local)], own_sem.at[0]),
        pltpu.make_async_copy(coeffs, cbuf.at[col], own_sem.at[1]),
    ]
    for j in range(2):
        local.append(
            pltpu.make_async_copy(
                slabs.at[j, :, pl.ds(pl.multiple_of(rows * half_of(me), rows), rows)],
                wbuf.at[me, j], own_sem.at[2 + j],
            )
        )
    for copy in local:
        copy.start()

    @pl.when(z == col)
    def _():
        copy = pltpu.make_async_copy(own_extra_src, ebuf.at[y], own_sem.at[4])
        copy.start()
        copy.wait()

    for copy in local:
        copy.wait()
    for step in range(1, n_z):
        source = lax.rem(z + step, n_z) * 2 + y
        copy = amp_copy(source, 0, beside, False)
        copy.wait_recv()
        copy.start()
        amp_sends.append(copy)
    for u in (0, 1):
        send_piece(z, u, start, True, (ACROSS,))
    send_extra(z, start, True)
    pl.when(end)(relay_other)

    def nth(n):
        low = z < n_z - 1 - z
        near = jnp.where(low, z, n_z - 1 - z)
        turn = jnp.where(near == 0, n, jnp.where(n == 0, near, jnp.where(n == 1, n_z - 1, 2 * (n - 2))))
        return jnp.where(low, turn, n_z - 1 - turn)

    def relay(n):
        source_z = nth(n)
        for u in (2, 3, 0, 1):
            w_copy(ACROSS, source_z * 2 + y, u, False).wait_recv()
            send_piece(source_z, u, start, False)
        pl.when(source_z == col)(lambda: e_copy(ACROSS, y, False).wait_recv())
        send_extra(source_z, start, False)

    relay(1)
    for step in range(n_z):
        amp_copy(lax.rem(z + step, n_z) * 2 + 1 - y, 0, beside, False).wait_recv()

    for j in range(2):
        for k in range(k_local):
            at = partner[j, me * k_local + k]
            pbuf[j * k_local + k, pl.ds(pl.multiple_of(mine * col, mine), mine), :] = abuf[at]

    my_rows = pl.ds(pl.multiple_of(mine * col, mine), mine)
    far_rows = pl.ds(pl.multiple_of(mine * opposite, mine), mine)

    def pick_copy(way):
        rows_of = my_rows if way < 2 else far_rows
        return remote(
            pbuf.at[:, rows_of], pbuf.at[:, rows_of],
            p_send.at[way], p_recv.at[way], me, (opposite, twin, twin)[way],
        )

    for way in range(2):
        pick_copy(way).start()

    for k in range(k_local):
        coeff_copy(k, 0).wait_recv()
        coeff_copy(k, 2).start()
    pl.when(jnp.logical_not(end))(relay_other)
    relay(2)
    pick_copy(0).wait_recv()
    pick_copy(2).start()
    for way in (1, 2):
        pick_copy(way).wait_recv()
    for j in range(2):
        for k in range(k_local):
            turned = pbuf[j * k_local + k].astype(jnp.float32).T.astype(jnp.bfloat16)
            xbuf[k, vectors * j : vectors * (j + 1), :] = turned
    proj[...] = jnp.zeros_like(proj)
    bacc[...] = jnp.zeros_like(bacc)
    for k in range(k_local):
        for way in (1, 2):
            coeff_copy(k, way).wait_recv()

    def coeff_rows(r, k):
        at = pl.ds(pl.multiple_of(rows * lax.rem(r, 2), rows), rows)
        return cbuf[lax.div(r, 2), k, at, :]

    @pl.loop(0, n_ka)
    def _(r):
        for k in range(k_local):
            both = nt(xbuf[k], coeff_rows(r, k)).astype(jnp.bfloat16)
            for j in range(2):
                dens[j, r, vectors * k : vectors * (k + 1), :] = both[vectors * j : vectors * (j + 1)]

    pl.when(jnp.logical_not(end))(lambda: relay(3))

    def project(part, r):
        low = part.astype(jnp.bfloat16)
        for k in range(k_local):
            proj[k] += nn(low[vectors * k : vectors * (k + 1)], coeff_rows(r, k))

    order = (0, 1, 0, 2, 1, 3, 2, 3)
    across = (0, 0, 1, 0, 1, 0, 1, 1)

    @pl.loop(0, n_ka)
    def _(i):
        @pl.when(end & (i == 4))
        def _():
            relay(3)

        source_z = nth(listed(i, order))
        other = listed(i, across)
        source = source_z * 2 + jnp.where(other == 1, 1 - y, y)

        @pl.when(other == 1)
        def _():
            wait_other(source_z)

        half = half_of(source)
        b = 2 * col + half
        part = nt(dens[0, b], wbuf[source, 0]) + nt(dens[1, b], wbuf[source, 1])

        @pl.when(source_z == col)
        def _():
            bacc[half] += part

        @pl.when(source_z != col)
        def _():
            project(part, source)
            bacc[half] += nn(dens[0, source], wbuf[source, 0]) + nn(dens[1, source], wbuf[source, 1])

    bacc[0] += nt(dens[0, 2 * col + 1], ebuf[0]) + nn(dens[1, 2 * col + 1], ebuf[1])
    bacc[1] += nn(dens[0, 2 * col], ebuf[0]) + nt(dens[1, 2 * col], ebuf[1])
    for half in range(2):
        project(bacc[half], 2 * col + half)

    for k in range(k_local):
        turned = proj[k].T.astype(jnp.bfloat16)
        for c in range(n_col):
            outgoing[c, k] = turned[mine * c : mine * (c + 1)]
    out_copies = []
    for step in range(1, n_col):
        to = lax.rem(col + step, n_col)
        copy = remote(
            outgoing.at[to], incoming.at[step], o_send.at[step], o_recv.at[step], me, to
        )
        copy.start()
        out_copies.append(copy)
    total = outgoing[col].astype(jnp.float32)
    for step, copy in enumerate(out_copies, 1):
        copy.wait_recv()
        total += incoming[step].astype(jnp.float32)
    out[...] = total

    for copy in amp_sends + out_copies:
        copy.wait_send()
    for way in range(3):
        pick_copy(way).wait_send()
        for k in range(k_local):
            coeff_copy(k, way).wait_send()
    sends(z, lambda copy: copy.wait_send(), True)
    for n in range(1, n_z):
        sends(nth(n), lambda copy: copy.wait_send(), False)
    sends_other(lambda copy: copy.wait_send())


def pick(qsel, w_screen, out, sem):
    copies = [
        pltpu.make_async_copy(w_screen.at[qsel[j]], out.at[j], sem.at[j]) for j in range(2)
    ]
    for copy in copies:
        copy.start()
    for copy in copies:
        copy.wait()


def body(n_ka, n_col, amps, isdf_coeffs, w_screen, energies, qsel, partner):
    k_local, mine, vectors = amps.shape
    pairs = isdf_coeffs.shape[2]
    rows, width = w_screen.shape[1:]
    vmem = pl.BlockSpec(memory_space=pltpu.VMEM)
    dma = pltpu.SemaphoreType.DMA
    bf16, f32 = jnp.bfloat16, jnp.float32
    slabs = pl.pallas_call(
        pick,
        out_shape=jax.ShapeDtypeStruct((2, rows, width), w_screen.dtype),
        in_specs=[pl.BlockSpec(memory_space=pltpu.SMEM), pl.BlockSpec(memory_space=pltpu.HBM)],
        out_specs=vmem,
        scratch_shapes=[dma((2,))],
    )(qsel, w_screen)
    summed = pl.pallas_call(
        functools.partial(kernel, n_ka, n_col),
        out_shape=jax.ShapeDtypeStruct(amps.shape, f32),
        in_specs=[pl.BlockSpec(memory_space=pltpu.SMEM)]
        + [pl.BlockSpec(memory_space=pl.ANY)] * 2
        + [pl.BlockSpec(memory_space=pltpu.HBM)],
        out_specs=vmem,
        scratch_shapes=[
            pltpu.VMEM((n_ka * k_local, mine, vectors), bf16),
            pltpu.VMEM((2 * k_local, pairs, vectors), bf16),
            pltpu.VMEM((n_col, k_local, width, pairs), bf16),
            pltpu.VMEM((n_ka, 2, rows, rows), bf16),
            pltpu.VMEM((2, rows, rows), bf16),
            pltpu.VMEM((k_local, 2 * vectors, pairs), bf16),
            pltpu.VMEM((2, n_ka, k_local * vectors, rows), bf16),
            pltpu.VMEM((2, k_local * vectors, rows), f32),
            pltpu.VMEM((k_local, vectors, pairs), f32),
            pltpu.VMEM((n_col, k_local, mine, vectors), bf16),
            pltpu.VMEM((n_col, k_local, mine, vectors), bf16),
            dma((n_ka, n_ka // 2)), dma((n_ka,)),
            dma((3,)), dma((3,)),
            dma((3, k_local)), dma((3, k_local)),
            dma((n_ka, 4, 5)), dma((n_ka, 4)),
            dma((2, 5)), dma((2,)),
            dma((n_col,)), dma((n_col,)),
            dma((5,)),
        ],
        compiler_params=pltpu.CompilerParams(
            collective_id=0, has_side_effects=True, vmem_limit_bytes=48 * 2**20
        ),
    )(partner, amps, isdf_coeffs, slabs)
    return summed + energies[:, :, None] * amps.astype(f32)


def solution(mesh):
    placed = (
        P("ka", "col", None),
        P("ka", "col", None),
        P(None, "ka", "col"),
        P("ka", "col"),
        P(),
        P(),
    )
    n_ka, n_col = mesh.shape["ka"], mesh.shape["col"]
    paired = n_ka == 2 * n_col and n_col == 4
    chosen = functools.partial(body, n_ka, n_col) if paired else general_body
    return jax.shard_map(
        chosen, mesh=mesh, in_specs=placed, out_specs=P("ka", "col", None), check_vma=False
    )
```

```python
import functools

import jax
import jax.numpy as jnp
from jax import lax
from jax.experimental import pallas as pl
from jax.experimental.pallas import tpu as pltpu
from jax.sharding import PartitionSpec as P

MESH = pl.DeviceIdType.MESH
ACROSS, UP, DOWN, UP2, DOWN2 = range(5)


def general_body(amps, isdf_coeffs, w_screen, energies, qsel, partner):
    k_local = amps.shape[0]
    vectors = amps.shape[2]
    offset_base = lax.axis_index("ka") * k_local
    owned = offset_base + jnp.arange(k_local, dtype=jnp.int32)
    wanted = jnp.take(partner, owned, axis=1).reshape(-1)
    everyone = lax.all_gather(amps, "ka", axis=0, tiled=True)
    picked = jnp.take(everyone, wanted, axis=0)
    partners = lax.all_gather(picked, "col", axis=1, tiled=True)
    partners = partners.reshape(2, k_local, partners.shape[1], vectors)
    densities = jnp.einsum(
        "kms,qkse->qmke", isdf_coeffs, partners, preferred_element_type=jnp.float32
    )
    width = densities.shape[1]
    densities = densities.astype(jnp.bfloat16).reshape(2, width, k_local * vectors)
    slabs = jnp.take(w_screen, qsel, axis=0)
    partials = jnp.einsum(
        "qrm,qmx->qrx",
        lax.all_gather(slabs, "ka", axis=1, tiled=True),
        densities,
        preferred_element_type=jnp.float32,
    )
    screened = lax.psum_scatter(
        partials.astype(jnp.bfloat16), "col", scatter_dimension=1, tiled=True
    ).astype(jnp.float32)
    screened = screened.astype(jnp.bfloat16).reshape(2, width, k_local, vectors)
    projected = jnp.einsum(
        "kms,qmke->kse", isdf_coeffs, screened, preferred_element_type=jnp.float32
    )
    summed = lax.psum_scatter(
        projected.astype(jnp.bfloat16), "col", scatter_dimension=1, tiled=True
    ).astype(jnp.float32)
    return summed + energies[:, :, None] * amps.astype(jnp.float32)


def listed(i, values):
    out = jnp.int32(values[0])
    for at, value in enumerate(values[1:], 1):
        out = jnp.where(i == at, jnp.int32(value), out)
    return out


def nt(a, b):
    return lax.dot_general(a, b, (((1,), (1,)), ((), ())), preferred_element_type=jnp.float32)


def nn(a, b):
    return jnp.dot(a, b, preferred_element_type=jnp.float32)


def kernel(
    n_ka, n_col, partner, amps, coeffs, slabs, out,
    abuf, pbuf, cbuf, wbuf, ebuf, xbuf, dens, bacc, proj, outgoing, incoming,
    a_send, a_recv, p_send, p_recv, c_send, c_recv, w_send, w_recv,
    e_send, e_recv, o_send, o_recv, own_sem,
):
    k_local, mine, vectors = amps.shape
    rows = slabs.shape[1]
    me = lax.axis_index("ka")
    col = lax.axis_index("col")
    n_z = n_ka // 2
    z, y = lax.div(me, 2), lax.rem(me, 2)
    beside = me + 1 - 2 * y
    twin = col + 1 - 2 * lax.rem(col, 2)
    opposite = lax.rem(col + 2, n_col)
    corner = lax.rem(twin + 2, n_col)

    def half_of(a):
        odd = lax.rem(a, 2)
        return jnp.where(a >= 2 * col, odd, 1 - odd)

    def remote(src, dst, send, recv, ka, at):
        return pltpu.make_async_remote_copy(
            src_ref=src, dst_ref=dst, send_sem=send, recv_sem=recv,
            device_id={"ka": ka, "col": at}, device_id_type=MESH,
        )

    barrier = pltpu.get_barrier_semaphore()
    for step in range(1, n_ka):
        pl.semaphore_signal(
            barrier, inc=1, device_id={"ka": lax.rem(me + step, n_ka), "col": col},
            device_id_type=MESH,
        )
    for step in range(1, n_col):
        pl.semaphore_signal(
            barrier, inc=1, device_id={"ka": me, "col": lax.rem(col + step, n_col)},
            device_id_type=MESH,
        )
    pl.semaphore_wait(barrier, n_ka + n_col - 2)

    def amp_copy(source, way, to, own):
        slot = abuf.at[pl.ds(source * k_local, k_local)]
        return remote(
            amps if own else slot, slot, a_send.at[source, way], a_recv.at[source], to, col
        )

    amp_sends = [amp_copy(me, 0, beside, True)]
    for step in range(1, n_z):
        amp_sends.append(amp_copy(me, step, lax.rem(z + step, n_z) * 2 + y, True))
    for copy in amp_sends:
        copy.start()

    def coeff_copy(k, way):
        to = (opposite, twin, twin)[way]
        src = coeffs.at[k] if way < 2 else cbuf.at[opposite, k]
        dst = cbuf.at[col if way < 2 else opposite, k]
        return remote(src, dst, c_send.at[way, k], c_recv.at[way, k], me, to)

    piece_rows = rows // 2

    def w_copy(way, source, u, own):
        to = (beside, me + 2, me - 2, me + 4, me - 4)[way]
        j, at = u // 2, pl.ds(u % 2 * piece_rows, piece_rows)
        dst = wbuf.at[source, j, at]
        if own:
            src = slabs.at[j, at, pl.ds(pl.multiple_of(rows * half_of(me), rows), rows)]
        else:
            src = dst
        return remote(src, dst, w_send.at[source, u, way], w_recv.at[source, u], to, col)

    own_extra_src = slabs.at[y, :, pl.ds(pl.multiple_of(rows * (1 - y), rows), rows)]

    def e_copy(way, j, own):
        to = (beside, me + 2, me - 2, me + 4, me - 4)[way]
        src = own_extra_src if own else ebuf.at[j]
        return remote(src, ebuf.at[j], e_send.at[j, way], e_recv.at[j], to, col)

    def across_first(source_z, j):
        return (source_z == 0) | (source_z == n_z - 1) if j == 1 else None

    def when(cond, act):
        if cond is None:
            act()
        else:
            pl.when(cond)(act)

    def along(source_z):
        first, after = source_z == z, source_z == z + 2
        before = source_z == z - 2
        return (
            (UP2, first & (z < n_z - 2)), (DOWN2, first & (z > 1)),
            (UP, (first | before) & (z < n_z - 1)), (DOWN, (first | after) & (z > 0)),
        )

    def send_piece(source_z, u, go, own, ways=range(5)):
        early = across_first(source_z, u // 2)
        over = None if own or early is None else jnp.logical_not(early)
        for way, wanted in ((ACROSS, over),) + along(source_z):
            if way in ways:
                when(wanted, lambda way=way: go(w_copy(way, source_z * 2 + y, u, own)))

    def send_extra(source_z, go, own):
        @pl.when(source_z == col)
        def _():
            for way, wanted in ((ACROSS, None),) + along(source_z):
                when(wanted, lambda way=way: go(e_copy(way, y, own)))

    def sends(source_z, go, own):
        for u in (2, 3, 0, 1):
            send_piece(source_z, u, go, own)
        send_extra(source_z, go, own)

    end = (z == 0) | (z == n_z - 1)
    passed = jnp.where(end, z, jnp.where(z < n_z - 1 - z, n_z - 1, 0))

    def sends_other(go):
        source = passed * 2 + 1 - y
        for u in (2, 3):
            for way, wanted in along(passed):
                when(wanted, lambda way=way, u=u: go(w_copy(way, source, u, False)))

    def relay_other():
        source = passed * 2 + 1 - y
        for u in (2, 3):
            w_copy(ACROSS, source, u, False).wait_recv()
            for way, wanted in along(passed):
                when(wanted, lambda way=way, u=u: w_copy(way, source, u, False).start())

    def wait_other(source_z):
        source = source_z * 2 + 1 - y
        for u in (0, 1):
            w_copy(ACROSS, source, u, False).wait_recv()

        @pl.when(source_z != passed)
        def _():
            for u in (2, 3):
                w_copy(ACROSS, source, u, False).wait_recv()

        pl.when(source_z == col)(lambda: e_copy(ACROSS, 1 - y, False).wait_recv())

    start = lambda copy: copy.start()
    for u in (2, 3):
        send_piece(z, u, start, True)
    for k in range(k_local):
        for way in range(2):
            coeff_copy(k, way).start()
    for u in (0, 1):
        send_piece(z, u, start, True, (UP, DOWN, UP2, DOWN2))

    local = [
        pltpu.make_async_copy(amps, abuf.at[pl.ds(me * k_local, k_local)], own_sem.at[0]),
        pltpu.make_async_copy(coeffs, cbuf.at[col], own_sem.at[1]),
    ]
    for j in range(2):
        local.append(
            pltpu.make_async_copy(
                slabs.at[j, :, pl.ds(pl.multiple_of(rows * half_of(me), rows), rows)],
                wbuf.at[me, j], own_sem.at[2 + j],
            )
        )
    for copy in local:
        copy.start()

    @pl.when(z == col)
    def _():
        copy = pltpu.make_async_copy(own_extra_src, ebuf.at[y], own_sem.at[4])
        copy.start()
        copy.wait()

    for copy in local:
        copy.wait()
    for step in range(1, n_z):
        source = lax.rem(z + step, n_z) * 2 + y
        copy = amp_copy(source, 0, beside, False)
        copy.wait_recv()
        copy.start()
        amp_sends.append(copy)
    for u in (0, 1):
        send_piece(z, u, start, True, (ACROSS,))
    send_extra(z, start, True)
    pl.when(end)(relay_other)

    def nth(n):
        low = z < n_z - 1 - z
        near = jnp.where(low, z, n_z - 1 - z)
        turn = jnp.where(near == 0, n, jnp.where(n == 0, near, jnp.where(n == 1, n_z - 1, 2 * (n - 2))))
        return jnp.where(low, turn, n_z - 1 - turn)

    def relay(n):
        source_z = nth(n)
        for u in (2, 3, 0, 1):
            w_copy(ACROSS, source_z * 2 + y, u, False).wait_recv()
            send_piece(source_z, u, start, False)
        pl.when(source_z == col)(lambda: e_copy(ACROSS, y, False).wait_recv())
        send_extra(source_z, start, False)

    for step in range(n_z):
        amp_copy(lax.rem(z + step, n_z) * 2 + 1 - y, 0, beside, False).wait_recv()

    for j in range(2):
        for k in range(k_local):
            at = partner[j, me * k_local + k]
            pbuf[j * k_local + k, pl.ds(pl.multiple_of(mine * col, mine), mine), :] = abuf[at]

    my_rows = pl.ds(pl.multiple_of(mine * col, mine), mine)
    far_rows = pl.ds(pl.multiple_of(mine * opposite, mine), mine)

    def pick_copy(way):
        rows_of = my_rows if way < 2 else far_rows
        return remote(
            pbuf.at[:, rows_of], pbuf.at[:, rows_of],
            p_send.at[way], p_recv.at[way], me, (opposite, twin, twin)[way],
        )

    for way in range(2):
        pick_copy(way).start()

    for k in range(k_local):
        coeff_copy(k, 0).wait_recv()
        coeff_copy(k, 2).start()
    relay(1)
    pick_copy(0).wait_recv()
    pick_copy(2).start()
    for way in (1, 2):
        pick_copy(way).wait_recv()
    for j in range(2):
        for k in range(k_local):
            turned = pbuf[j * k_local + k].astype(jnp.float32).T.astype(jnp.bfloat16)
            xbuf[k, vectors * j : vectors * (j + 1), :] = turned
    proj[...] = jnp.zeros_like(proj)
    bacc[...] = jnp.zeros_like(bacc)
    for k in range(k_local):
        for way in (1, 2):
            coeff_copy(k, way).wait_recv()

    def coeff_rows(r, k):
        at = pl.ds(pl.multiple_of(rows * lax.rem(r, 2), rows), rows)
        return cbuf[lax.div(r, 2), k, at, :]

    @pl.loop(0, n_ka)
    def _(r):
        for k in range(k_local):
            both = nt(xbuf[k], coeff_rows(r, k)).astype(jnp.bfloat16)
            for j in range(2):
                dens[j, r, vectors * k : vectors * (k + 1), :] = both[vectors * j : vectors * (j + 1)]

    pl.when(jnp.logical_not(end))(relay_other)
    relay(2)
    pl.when(jnp.logical_not(end))(lambda: relay(3))

    def project(part, r):
        low = part.astype(jnp.bfloat16)
        for k in range(k_local):
            proj[k] += nn(low[vectors * k : vectors * (k + 1)], coeff_rows(r, k))

    order = (0, 1, 0, 2, 1, 3, 2, 3)
    across = (0, 0, 1, 0, 1, 0, 1, 1)

    @pl.loop(0, n_ka)
    def _(i):
        @pl.when(end & (i == 4))
        def _():
            relay(3)

        source_z = nth(listed(i, order))
        other = listed(i, across)
        source = source_z * 2 + jnp.where(other == 1, 1 - y, y)

        @pl.when(other == 1)
        def _():
            wait_other(source_z)

        half = half_of(source)
        b = 2 * col + half
        part = nt(dens[0, b], wbuf[source, 0]) + nt(dens[1, b], wbuf[source, 1])

        @pl.when(source_z == col)
        def _():
            bacc[half] += part

        @pl.when(source_z != col)
        def _():
            project(part, source)
            bacc[half] += nn(dens[0, source], wbuf[source, 0]) + nn(dens[1, source], wbuf[source, 1])

    bacc[0] += nt(dens[0, 2 * col + 1], ebuf[0]) + nn(dens[1, 2 * col + 1], ebuf[1])
    bacc[1] += nn(dens[0, 2 * col], ebuf[0]) + nt(dens[1, 2 * col], ebuf[1])
    for half in range(2):
        project(bacc[half], 2 * col + half)

    for k in range(k_local):
        turned = proj[k].T.astype(jnp.bfloat16)
        for c in range(n_col):
            outgoing[c, k] = turned[mine * c : mine * (c + 1)]
    out_copies = []
    for step in range(1, n_col):
        to = lax.rem(col + step, n_col)
        copy = remote(
            outgoing.at[to], incoming.at[step], o_send.at[step], o_recv.at[step], me, to
        )
        copy.start()
        out_copies.append(copy)
    total = outgoing[col].astype(jnp.float32)
    for step, copy in enumerate(out_copies, 1):
        copy.wait_recv()
        total += incoming[step].astype(jnp.float32)
    out[...] = total

    for copy in amp_sends + out_copies:
        copy.wait_send()
    for way in range(3):
        pick_copy(way).wait_send()
        for k in range(k_local):
            coeff_copy(k, way).wait_send()
    sends(z, lambda copy: copy.wait_send(), True)
    for n in range(1, n_z):
        sends(nth(n), lambda copy: copy.wait_send(), False)
    sends_other(lambda copy: copy.wait_send())


def pick(qsel, w_screen, out, held, sem):
    into = [pltpu.make_async_copy(w_screen.at[qsel[j]], held.at[j], sem.at[0, j]) for j in range(2)]
    away = [pltpu.make_async_copy(held.at[j], out.at[j], sem.at[1, j]) for j in range(2)]
    for copy in into:
        copy.start()
    for j in range(2):
        into[j].wait()
        away[j].start()
    for copy in away:
        copy.wait()


def body(n_ka, n_col, amps, isdf_coeffs, w_screen, energies, qsel, partner):
    k_local, mine, vectors = amps.shape
    pairs = isdf_coeffs.shape[2]
    rows, width = w_screen.shape[1:]
    vmem = pl.BlockSpec(memory_space=pltpu.VMEM)
    dma = pltpu.SemaphoreType.DMA
    bf16, f32 = jnp.bfloat16, jnp.float32
    slabs = pl.pallas_call(
        pick,
        out_shape=jax.ShapeDtypeStruct((2, rows, width), w_screen.dtype),
        in_specs=[pl.BlockSpec(memory_space=pltpu.SMEM), pl.BlockSpec(memory_space=pltpu.HBM)],
        out_specs=pl.BlockSpec(memory_space=pltpu.HBM),
        scratch_shapes=[pltpu.VMEM((2, rows, width), w_screen.dtype), dma((2, 2))],
    )(qsel, w_screen)
    summed = pl.pallas_call(
        functools.partial(kernel, n_ka, n_col),
        out_shape=jax.ShapeDtypeStruct(amps.shape, f32),
        in_specs=[pl.BlockSpec(memory_space=pltpu.SMEM)]
        + [pl.BlockSpec(memory_space=pl.ANY)] * 2
        + [pl.BlockSpec(memory_space=pltpu.HBM)],
        out_specs=vmem,
        scratch_shapes=[
            pltpu.VMEM((n_ka * k_local, mine, vectors), bf16),
            pltpu.VMEM((2 * k_local, pairs, vectors), bf16),
            pltpu.VMEM((n_col, k_local, width, pairs), bf16),
            pltpu.VMEM((n_ka, 2, rows, rows), bf16),
            pltpu.VMEM((2, rows, rows), bf16),
            pltpu.VMEM((k_local, 2 * vectors, pairs), bf16),
            pltpu.VMEM((2, n_ka, k_local * vectors, rows), bf16),
            pltpu.VMEM((2, k_local * vectors, rows), f32),
            pltpu.VMEM((k_local, vectors, pairs), f32),
            pltpu.VMEM((n_col, k_local, mine, vectors), bf16),
            pltpu.VMEM((n_col, k_local, mine, vectors), bf16),
            dma((n_ka, n_ka // 2)), dma((n_ka,)),
            dma((3,)), dma((3,)),
            dma((3, k_local)), dma((3, k_local)),
            dma((n_ka, 4, 5)), dma((n_ka, 4)),
            dma((2, 5)), dma((2,)),
            dma((n_col,)), dma((n_col,)),
            dma((5,)),
        ],
        compiler_params=pltpu.CompilerParams(
            collective_id=0, has_side_effects=True, vmem_limit_bytes=48 * 2**20
        ),
    )(partner, amps, isdf_coeffs, slabs)
    return summed + energies[:, :, None] * amps.astype(f32)


def solution(mesh):
    placed = (
        P("ka", "col", None),
        P("ka", "col", None),
        P(None, "ka", "col"),
        P("ka", "col"),
        P(),
        P(),
    )
    n_ka, n_col = mesh.shape["ka"], mesh.shape["col"]
    paired = n_ka == 2 * n_col and n_col == 4
    chosen = functools.partial(body, n_ka, n_col) if paired else general_body
    return jax.shard_map(
        chosen, mesh=mesh, in_specs=placed, out_specs=P("ka", "col", None), check_vma=False
    )
```
